32 devices in a mesh: pipe: 4 (over x, core), sp: 2 (over y), dp: 4 (over z).
Axes of the slice: x: 2, y: 2, z: 4, core: 2. Of those that a mesh axis runs over, the one named last changes fastest.
Arguments:
- fresh_input: bfloat16 [4, 4, 120, 240, 128], P('pipe', 'dp', 'sp'), may hold values from -6 to 6
- saved_input: bfloat16 [4, 4, 120, 240, 128], P('pipe', 'dp', 'sp'), may hold values from -6 to 6
- output_grad: bfloat16 [4, 4, 120, 240, 128], P('pipe', 'dp', 'sp'), may hold values from -6 to 6
- expand_weight: bfloat16 [4, 128, 768], P('pipe'), may hold values from -0.5 to 0.5
- reduce_weight: bfloat16 [4, 768, 128], P('pipe'), may hold values from -0.21875 to 0.21875
- filter_weight: float32 [4, 2, 120, 128], P('pipe'), may hold values from -6 to 6
- cycle_table: int32 [120], replicated, may hold values from 0 to 119, each once
Outputs:
- next_input: bfloat16 [4, 4, 120, 240, 128], P('pipe', 'dp', 'sp')
- input_grad: bfloat16 [4, 4, 120, 240, 128], P('pipe', 'dp', 'sp')
- expand_grad: float32 [4, 128, 768], P('pipe', None, 'dp')
- reduce_grad: float32 [4, 768, 128], P('pipe', 'dp')
- filter_grad: float32 [4, 2, 120, 128], P('pipe')
The draws below stay inside these ranges and needn't reach their ends.
Inputs may be any that keep to these rules, and one draw needn't show every extreme that they name: `cycle_table`: each of 0 .. 119 appears once; values 120 or more mark empty cycle slots.
All inputs are finite; a program needn't handle non-finite values.
Results may differ from the reference program's by a relative error of at most 0.025.
Values may be sent and summed in bfloat16 or wider, within the bound.
A program may use at most 192 MiB of HBM per device.

```python
import math
import jax
import jax.numpy as jnp
from jax import lax

NLAT = 120
NLON = 240
CH = 128
HID = 768
SECTIONS = 4
GROUPS = 4
SLOTS_ALL = 120


def block_scale(stream_key, dims, split, low, top_value):
    level = 1.0
    for axis_at, shards_of in split:
        draws = jax.random.uniform(jax.random.fold_in(jax.random.fold_in(stream_key, 6), axis_at), (shards_of,), jnp.float32, low / len(split), top_value / len(split))
        level = level * jnp.repeat(jnp.exp(draws), dims[axis_at] // shards_of).reshape((-1,) + (1,) * (len(dims) - 1 - axis_at))
    return level


def bell_draw(stream_key, dims, spread, most, pieces=(), kind=jnp.bfloat16):
    array = spread * jax.random.normal(stream_key, dims, jnp.float32)
    if pieces:
        array = array * block_scale(stream_key, dims, pieces, -0.22, 0.18)
    return jnp.clip(array, -most, most).astype(kind)


def setup_inputs(seed: int = 0) -> dict:
    keys = jax.random.split(jax.random.key(seed), 8)
    return {
        "fresh_input": bell_draw(keys[0], (SECTIONS, GROUPS, SLOTS_ALL, NLON, CH), 1.0, 6.0, ((0, 4), (1, 4), (2, 2))),
        "saved_input": bell_draw(keys[1], (SECTIONS, GROUPS, SLOTS_ALL, NLON, CH), 1.0, 6.0, ((0, 4), (1, 4), (2, 2))),
        "output_grad": bell_draw(keys[2], (SECTIONS, GROUPS, SLOTS_ALL, NLON, CH), 1.0, 6.0, ((0, 4), (1, 4), (2, 2))),
        "expand_weight": bell_draw(keys[3], (SECTIONS, CH, HID), CH ** -0.5, 0.5, ((0, 4),)),
        "reduce_weight": bell_draw(keys[4], (SECTIONS, HID, CH), HID ** -0.5, 0.21875, ((0, 4),)),
        "filter_weight": bell_draw(keys[5], (SECTIONS, 2, NLAT, CH), 1.0, 6.0, ((0, 4),), jnp.float32),
        "cycle_table": jax.random.permutation(keys[6], SLOTS_ALL).astype(jnp.int32),
    }


ROOT_HALF = 0.7071067811865476
INV_ROOT_TAU = 0.3989422804014327

def gelu_value(pre_act):
    return 0.5 * pre_act * (1.0 + lax.erf(pre_act * ROOT_HALF))

def gelu_slope(pre_act):
    return 0.5 * (1.0 + lax.erf(pre_act * ROOT_HALF)) + pre_act * jnp.exp(-0.5 * pre_act * pre_act) * INV_ROOT_TAU

def legendre(lat_index, order_index, cycles):
    lat_ok = (lat_index < cycles).astype(jnp.float32)
    order_ok = (order_index < cycles).astype(jnp.float32)
    colatitude = math.pi * (jnp.minimum(lat_index, cycles - 1).astype(jnp.float32) + 0.5) / cycles
    cosine = jnp.cos(colatitude)[None, :]
    sine_value = jnp.sin(colatitude)[None, :]
    order_value = jnp.minimum(order_index, cycles - 1).astype(jnp.float32)[:, None]
    log_start = 0.5 * (jnp.log((2.0 * order_value + 1.0) / (4.0 * math.pi)) + lax.lgamma(2.0 * order_value + 1.0) - 2.0 * lax.lgamma(order_value + 1.0) - order_value * math.log(4.0)) + order_value * jnp.log(sine_value)
    starting = jnp.exp(log_start)
    zero_rows = jnp.zeros_like(starting)

    def advance(state_pair, degree):
        previous, earlier = state_pair
        degree_value = degree.astype(jnp.float32)
        upper_term = jnp.maximum(4.0 * degree_value * degree_value - 1.0, 0.0)
        ratio_main = jnp.sqrt(upper_term / jnp.maximum(degree_value * degree_value - order_value * order_value, 1.0))
        ratio_back = jnp.sqrt(jnp.maximum((degree_value - 1.0) ** 2 - order_value * order_value, 0.0) / jnp.maximum(4.0 * (degree_value - 1.0) ** 2 - 1.0, 1.0))
        rising = ratio_main * (cosine * previous - ratio_back * earlier)
        current = jnp.where(degree_value == order_value, starting, jnp.where(degree_value > order_value, rising, 0.0))
        return ((current, previous), current)
    _, stacked = lax.scan(advance, (zero_rows, zero_rows), jnp.arange(cycles, dtype=jnp.int32))
    valid_mask = order_ok[:, None] * lat_ok[None, :]
    return jnp.transpose(stacked, (1, 0, 2)) * valid_mask[:, None, :]

def cycle_weights(lat_index, cycles):
    valid_cycle = (lat_index < cycles).astype(jnp.float32)
    colatitude = math.pi * (jnp.minimum(lat_index, cycles - 1).astype(jnp.float32) + 0.5) / cycles
    return math.pi / cycles * jnp.sin(colatitude) * valid_cycle

def fourier_tables(order_index, cycles, points):
    valid_order = (order_index < cycles).astype(jnp.float32)[None, :]
    order_value = jnp.minimum(order_index, cycles - 1).astype(jnp.int32)
    longitude = jnp.arange(points, dtype=jnp.int32)
    phase_angle = 2.0 * math.pi / points * (longitude[:, None] * order_value[None, :] % points).astype(jnp.float32)
    scaled = valid_order * (2.0 * math.pi / points)
    forward = jnp.concatenate([jnp.cos(phase_angle) * scaled, -jnp.sin(phase_angle) * scaled], axis=1)
    order_scale = jnp.where(order_value == 0, 1.0, 2.0)[None, :] * valid_order / (2.0 * math.pi)
    inverse = jnp.concatenate([jnp.cos(phase_angle) * order_scale, -jnp.sin(phase_angle) * order_scale], axis=1).T
    return (forward.astype(jnp.bfloat16), inverse.astype(jnp.bfloat16))

def spectral_pass(tokens, filt, forward, analysis, synthesis, inverse):
    row_count, points, chan_count = tokens.shape
    order_count = synthesis.shape[0]
    coeffs = jnp.einsum('jnc,nk->jkc', tokens.astype(jnp.float32), forward.astype(jnp.float32)).astype(jnp.bfloat16)
    coeffs = coeffs.reshape(row_count, 2, order_count, chan_count)
    spectra = jnp.einsum('tlj,jrtc->trlc', analysis.astype(jnp.float32), coeffs.astype(jnp.float32))
    real_part = filt[0] * spectra[:, 0] - filt[1] * spectra[:, 1]
    imag_part = filt[0] * spectra[:, 1] + filt[1] * spectra[:, 0]
    filtered = jnp.stack([real_part, imag_part], axis=1).astype(jnp.bfloat16)
    values = jnp.einsum('tlj,trlc->jrtc', synthesis.astype(jnp.float32), filtered.astype(jnp.float32)).astype(jnp.bfloat16)
    values = values.reshape(row_count, 2 * order_count, chan_count)
    spatial = jnp.einsum('jkc,kn->jnc', values.astype(jnp.float32), inverse.astype(jnp.float32))
    return (spatial, spectra)

def mlp_pass(tokens, spatial, expand, contract, cycle_mask):
    grid_shape = tokens.shape
    flat_rows = (tokens.astype(jnp.float32) + spatial).reshape(-1, grid_shape[-1])
    mixed_b = flat_rows.astype(jnp.bfloat16)
    hidden_pre = jnp.dot(mixed_b, expand, preferred_element_type=jnp.float32)
    hidden = gelu_value(hidden_pre).astype(jnp.bfloat16)
    result = flat_rows + jnp.dot(hidden, contract, preferred_element_type=jnp.float32)
    result = (result.reshape(grid_shape) * cycle_mask[:, None, None]).astype(jnp.bfloat16)
    return (result, mixed_b, hidden_pre, hidden)

def backward_rows(cotangent, cycle_mask, mixed_b, hidden_pre, hidden, expand, contract):
    chan_count = cotangent.shape[-1]
    masked = (cotangent * cycle_mask.astype(jnp.bfloat16)[:, None, None]).reshape(-1, chan_count)
    grad_reduce = jnp.dot(hidden.T, masked, preferred_element_type=jnp.float32)
    grad_hidden = jnp.dot(masked, contract.T, preferred_element_type=jnp.float32)
    grad_pre = (grad_hidden * gelu_slope(hidden_pre)).astype(jnp.bfloat16)
    grad_expand = jnp.dot(mixed_b.T, grad_pre, preferred_element_type=jnp.float32)
    grad_mixed = masked.astype(jnp.float32) + jnp.dot(grad_pre, expand.T, preferred_element_type=jnp.float32)
    return (grad_mixed, grad_expand, grad_reduce)

def spectral_back(grad_mixed, spectra, filt, forward, inverse, analysis, synthesis, grid_shape):
    row_count, points, chan_count = grid_shape
    order_count = synthesis.shape[0]
    grad_rows = grad_mixed.reshape(grid_shape).astype(jnp.bfloat16)
    grad_values = jnp.einsum('jnc,kn->jkc', grad_rows.astype(jnp.float32), inverse.astype(jnp.float32)).astype(jnp.bfloat16)
    grad_values = grad_values.reshape(row_count, 2, order_count, chan_count)
    grad_filtered = jnp.einsum('tlj,jrtc->trlc', synthesis.astype(jnp.float32), grad_values.astype(jnp.float32))
    filter_real = lax.optimization_barrier(jnp.sum(grad_filtered[:, 0] * spectra[:, 0] + grad_filtered[:, 1] * spectra[:, 1], axis=0))
    filter_imag = lax.optimization_barrier(jnp.sum(grad_filtered[:, 1] * spectra[:, 0] - grad_filtered[:, 0] * spectra[:, 1], axis=0))
    grad_spectra = jnp.stack([filt[0] * grad_filtered[:, 0] + filt[1] * grad_filtered[:, 1], filt[0] * grad_filtered[:, 1] - filt[1] * grad_filtered[:, 0]], axis=1).astype(jnp.bfloat16)
    grad_coeffs = jnp.einsum('tlj,trlc->jrtc', analysis.astype(jnp.float32), grad_spectra.astype(jnp.float32)).astype(jnp.bfloat16)
    grad_coeffs = grad_coeffs.reshape(row_count, 2 * order_count, chan_count)
    grad_tokens = jnp.einsum('jkc,nk->jnc', grad_coeffs.astype(jnp.float32), forward.astype(jnp.float32))
    return (grad_tokens, jnp.stack([filter_real, filter_imag]))

def reference(fresh_input, saved_input, output_grad, expand_weight, reduce_weight, filter_weight, cycle_table):
    order_table = jnp.arange(SLOTS_ALL, dtype=jnp.int32)
    table = legendre(cycle_table, order_table, NLAT)
    analysis = (table * cycle_weights(cycle_table, NLAT)[None, None, :]).astype(jnp.bfloat16)
    synthesis = table.astype(jnp.bfloat16)
    forward, inverse = fourier_tables(order_table, NLAT, NLON)
    cycle_mask = (cycle_table < NLAT).astype(jnp.float32)
    zero_block = jnp.zeros(fresh_input.shape[2:], jnp.bfloat16)
    next_rows = [[zero_block] * GROUPS]
    for section in range(1, SECTIONS):
        members = []
        for member in range(GROUPS):
            tokens = fresh_input[section - 1, member]
            spatial, _ = spectral_pass(tokens, filter_weight[section - 1], forward, analysis, synthesis, inverse)
            members.append(mlp_pass(tokens, spatial, expand_weight[section - 1], reduce_weight[section - 1], cycle_mask)[0])
        next_rows.append(members)
    grad_rows = []
    expand_list, reduce_list, filter_list = ([], [], [])
    for section in range(SECTIONS):
        filt = filter_weight[section]
        expand_total = jnp.zeros(expand_weight.shape[1:], jnp.float32)
        reduce_total = jnp.zeros(reduce_weight.shape[1:], jnp.float32)
        filter_total = jnp.zeros(filter_weight.shape[1:], jnp.float32)
        members = []
        for member in range(GROUPS):
            tokens = saved_input[section, member]
            spatial, spectra = spectral_pass(tokens, filt, forward, analysis, synthesis, inverse)
            _, mixed_b, hidden_pre, hidden = mlp_pass(tokens, spatial, expand_weight[section], reduce_weight[section], cycle_mask)
            grad_mixed, grad_expand, grad_reduce = backward_rows(output_grad[section, member], cycle_mask, mixed_b, hidden_pre, hidden, expand_weight[section], reduce_weight[section])
            grad_tokens, filter_part = spectral_back(grad_mixed, spectra, filt, forward, inverse, analysis, synthesis, tokens.shape)
            members.append(((grad_mixed.reshape(tokens.shape) + grad_tokens) * cycle_mask[:, None, None]).astype(jnp.bfloat16))
            expand_total = expand_total + grad_expand
            reduce_total = reduce_total + grad_reduce
            filter_total = filter_total + filter_part
        if section > 0:
            grad_rows.append(members)
        expand_list.append(expand_total)
        reduce_list.append(reduce_total)
        filter_list.append(filter_total)
    grad_rows.append([zero_block] * GROUPS)
    next_input = jnp.stack([jnp.stack(group_row) for group_row in next_rows])
    input_grad = jnp.stack([jnp.stack(group_row) for group_row in grad_rows])
    return (next_input, input_grad, jnp.stack(expand_list), jnp.stack(reduce_list), jnp.stack(filter_list))
```

```python
import functools
import math

import jax
import jax.numpy as jnp
from jax import lax
from jax.experimental import pallas as pl
from jax.experimental.pallas import tpu as pltpu
from jax.sharding import PartitionSpec as P

NLAT = 120
NLON = 240


ROOT_HALF = 0.7071067811865476
INV_ROOT_TAU = 0.3989422804014327


def from_behind(block, axis, distance):
    devices = range(lax.axis_size(axis))
    route = [(i - distance, i) for i in devices if i - distance in devices]
    return lax.ppermute(block, axis, route)


def gelu_value(pre_act):
    return 0.5 * pre_act * (1.0 + lax.erf(pre_act * ROOT_HALF))


def gelu_slope(pre_act):
    return (
        0.5 * (1.0 + lax.erf(pre_act * ROOT_HALF))
        + pre_act * jnp.exp(-0.5 * pre_act * pre_act) * INV_ROOT_TAU
    )


def legendre(lat_index, order_index, cycles):
    lat_ok = (lat_index < cycles).astype(jnp.float32)
    order_ok = (order_index < cycles).astype(jnp.float32)
    colatitude = math.pi * (jnp.minimum(lat_index, cycles - 1).astype(jnp.float32) + 0.5) / cycles
    cosine = jnp.cos(colatitude)[None, :]
    sine_value = jnp.sin(colatitude)[None, :]
    order_value = jnp.minimum(order_index, cycles - 1).astype(jnp.float32)[:, None]
    log_start = 0.5 * (
        jnp.log((2.0 * order_value + 1.0) / (4.0 * math.pi))
        + lax.lgamma(2.0 * order_value + 1.0)
        - 2.0 * lax.lgamma(order_value + 1.0)
        - order_value * math.log(4.0)
    ) + order_value * jnp.log(sine_value)
    starting = jnp.exp(log_start)
    zero_rows = jnp.zeros_like(starting)

    def advance(state_pair, degree):
        previous, earlier = state_pair
        degree_value = degree.astype(jnp.float32)
        upper_term = jnp.maximum(4.0 * degree_value * degree_value - 1.0, 0.0)
        ratio_main = jnp.sqrt(
            upper_term / jnp.maximum(degree_value * degree_value - order_value * order_value, 1.0)
        )
        ratio_back = jnp.sqrt(
            jnp.maximum((degree_value - 1.0) ** 2 - order_value * order_value, 0.0)
            / jnp.maximum(4.0 * (degree_value - 1.0) ** 2 - 1.0, 1.0)
        )
        rising = ratio_main * (cosine * previous - ratio_back * earlier)
        current = jnp.where(
            degree_value == order_value,
            starting,
            jnp.where(degree_value > order_value, rising, 0.0),
        )
        return ((current, previous), current)

    _, stacked = lax.scan(advance, (zero_rows, zero_rows), jnp.arange(cycles, dtype=jnp.int32))
    valid_mask = order_ok[:, None] * lat_ok[None, :]
    return jnp.transpose(stacked, (1, 0, 2)) * valid_mask[:, None, :]


def cycle_weights(lat_index, cycles):
    valid_cycle = (lat_index < cycles).astype(jnp.float32)
    colatitude = math.pi * (jnp.minimum(lat_index, cycles - 1).astype(jnp.float32) + 0.5) / cycles
    return math.pi / cycles * jnp.sin(colatitude) * valid_cycle


def fourier_tables(order_index, cycles, points):
    valid_order = (order_index < cycles).astype(jnp.float32)[None, :]
    order_value = jnp.minimum(order_index, cycles - 1)
    longitude = jnp.arange(points, dtype=jnp.int32)
    phase_angle = (
        2.0
        * math.pi
        / points
        * (longitude[:, None] * order_value[None, :] % points).astype(jnp.float32)
    )
    scaled = valid_order * (2.0 * math.pi / points)
    forward = jnp.concatenate(
        [jnp.cos(phase_angle) * scaled, -jnp.sin(phase_angle) * scaled], axis=1
    )
    order_scale = jnp.where(order_value == 0, 1.0, 2.0)[None, :] * valid_order / (2.0 * math.pi)
    inverse = jnp.concatenate(
        [jnp.cos(phase_angle) * order_scale, -jnp.sin(phase_angle) * order_scale], axis=1
    ).T
    return (forward.astype(jnp.bfloat16), inverse.astype(jnp.bfloat16))


def joint_orders(coeffs):
    return lax.all_to_all(coeffs, "sp", split_axis=3, concat_axis=1, tiled=True)


def joint_cycles(values):
    return lax.all_to_all(values, "sp", split_axis=1, concat_axis=3, tiled=True)


def spectral_pass(tokens, filt, forward, analysis, synthesis, inverse, to_orders, to_cycles):
    batch_count, row_count, points, chan_count = tokens.shape
    order_count = forward.shape[1] // 2
    coeffs = jnp.einsum(
        "sjnc,nk->sjkc", tokens, forward, preferred_element_type=jnp.float32
    ).astype(jnp.bfloat16)
    coeffs = coeffs.reshape(batch_count, row_count, 2, order_count, chan_count)
    arrived = to_orders(coeffs)
    spectra = jnp.einsum("tlj,sjrtc->strlc", analysis, arrived, preferred_element_type=jnp.float32)
    real_part = filt[0] * spectra[:, :, 0] - filt[1] * spectra[:, :, 1]
    imag_part = filt[0] * spectra[:, :, 1] + filt[1] * spectra[:, :, 0]
    filtered = jnp.stack([real_part, imag_part], axis=2).astype(jnp.bfloat16)
    values = jnp.einsum(
        "tlj,strlc->sjrtc", synthesis, filtered, preferred_element_type=jnp.float32
    ).astype(jnp.bfloat16)
    returned = to_cycles(values).reshape(batch_count, row_count, 2 * order_count, chan_count)
    spatial = jnp.einsum("sjkc,kn->sjnc", returned, inverse, preferred_element_type=jnp.float32)
    return (spatial, spectra)


def mlp_pass(tokens, spatial, expand, contract, cycle_mask):
    grid_shape = tokens.shape
    flat_rows = (tokens.astype(jnp.float32) + spatial).reshape(-1, grid_shape[-1])
    mixed_b = flat_rows.astype(jnp.bfloat16)
    hidden_pre = jnp.dot(mixed_b, expand, preferred_element_type=jnp.float32)
    hidden = gelu_value(hidden_pre).astype(jnp.bfloat16)
    result = flat_rows + jnp.dot(hidden, contract, preferred_element_type=jnp.float32)
    result = (result.reshape(grid_shape) * cycle_mask[:, None, None]).astype(jnp.bfloat16)
    return (result, mixed_b, hidden_pre, hidden)


def backward_rows(cotangent, cycle_mask, mixed_b, hidden_pre, hidden, expand, contract):
    chan_count = cotangent.shape[-1]
    masked = (cotangent * cycle_mask.astype(jnp.bfloat16)[:, None, None]).reshape(-1, chan_count)
    grad_reduce = jnp.dot(hidden.T, masked, preferred_element_type=jnp.float32)
    grad_hidden = jnp.dot(masked, contract.T, preferred_element_type=jnp.float32)
    grad_pre = (grad_hidden * gelu_slope(hidden_pre)).astype(jnp.bfloat16)
    grad_expand = jnp.dot(mixed_b.T, grad_pre, preferred_element_type=jnp.float32)
    grad_mixed = masked.astype(jnp.float32) + jnp.dot(
        grad_pre, expand.T, preferred_element_type=jnp.float32
    )
    return (grad_mixed, grad_expand, grad_reduce)


def on_device(
    fresh_input, saved_input, output_grad, expand_weight, reduce_weight, filter_weight, cycle_table
):
    slot_count = fresh_input.shape[2]
    position = lax.axis_index("sp")
    order_table = jnp.arange(slot_count * lax.axis_size("sp"), dtype=jnp.int32)
    own_cycles = lax.dynamic_slice_in_dim(cycle_table, position * slot_count, slot_count)
    own_orders = lax.dynamic_slice_in_dim(order_table, position * slot_count, slot_count)
    cycle_mask = (own_cycles < NLAT).astype(jnp.float32)
    table = legendre(cycle_table, own_orders, NLAT)
    analysis = (table * cycle_weights(cycle_table, NLAT)[None, None, :]).astype(jnp.bfloat16)
    synthesis = table.astype(jnp.bfloat16)
    forward, inverse = fourier_tables(order_table, NLAT, NLON)
    filt = filter_weight[0]
    expand = expand_weight[0]
    contract = reduce_weight[0]
    fresh = fresh_input[0, 0]
    saved = saved_input[0, 0]
    spatial, spectra = spectral_pass(
        jnp.stack([fresh, saved]),
        filt,
        forward,
        analysis,
        synthesis,
        inverse,
        joint_orders,
        joint_cycles,
    )
    fresh_spatial = spatial[0]
    saved_spatial = spatial[1]
    saved_spectra = spectra[1]
    block = mlp_pass(fresh, fresh_spatial, expand, contract, cycle_mask)[0]
    next_input = from_behind(block[None, None], "pipe", 1)
    _, mixed_b, hidden_pre, hidden = mlp_pass(saved, saved_spatial, expand, contract, cycle_mask)
    grad_mixed, grad_expand, grad_reduce = backward_rows(
        output_grad[0, 0], cycle_mask, mixed_b, hidden_pre, hidden, expand, contract
    )
    grid_shape = saved.shape
    row_count, points, chan_count = grid_shape
    order_count = forward.shape[1] // 2
    grad_rows = grad_mixed.reshape(grid_shape).astype(jnp.bfloat16)
    grad_values = jnp.einsum(
        "jnc,kn->jkc", grad_rows, inverse, preferred_element_type=jnp.float32
    ).astype(jnp.bfloat16)
    grad_values = grad_values.reshape(row_count, 2, order_count, chan_count)
    arrived = lax.all_to_all(grad_values, "sp", split_axis=2, concat_axis=0, tiled=True)
    grad_filtered = jnp.einsum(
        "tlj,jrtc->trlc", synthesis, arrived, preferred_element_type=jnp.float32
    )
    filter_real = jnp.sum(
        grad_filtered[:, 0] * saved_spectra[:, 0] + grad_filtered[:, 1] * saved_spectra[:, 1],
        axis=0,
    )
    filter_imag = jnp.sum(
        grad_filtered[:, 1] * saved_spectra[:, 0] - grad_filtered[:, 0] * saved_spectra[:, 1],
        axis=0,
    )
    grad_spectra = jnp.stack(
        [
            filt[0] * grad_filtered[:, 0] + filt[1] * grad_filtered[:, 1],
            filt[0] * grad_filtered[:, 1] - filt[1] * grad_filtered[:, 0],
        ],
        axis=1,
    ).astype(jnp.bfloat16)
    grad_coeffs = jnp.einsum(
        "tlj,trlc->jrtc", analysis, grad_spectra, preferred_element_type=jnp.float32
    ).astype(jnp.bfloat16)
    returned = lax.all_to_all(grad_coeffs, "sp", split_axis=0, concat_axis=2, tiled=True)
    grad_tokens = jnp.einsum(
        "jkc,nk->jnc",
        returned.reshape(row_count, 2 * order_count, chan_count),
        forward,
        preferred_element_type=jnp.float32,
    )
    input_grad = (
        (grad_mixed.reshape(grid_shape) + grad_tokens) * cycle_mask[:, None, None]
    ).astype(jnp.bfloat16)
    sent_back = from_behind(input_grad[None, None], "pipe", -1)
    filter_grad = lax.psum(jnp.stack([filter_real, filter_imag]), ("sp", "dp"))
    summed = (
        lax.psum(grad_expand.astype(jnp.bfloat16), "sp").astype(jnp.float32),
        lax.psum(grad_reduce.astype(jnp.bfloat16), "sp").astype(jnp.float32),
    )
    expand_grad, reduce_grad = (
        lax.psum_scatter(
            summed[0].astype(jnp.bfloat16), "dp", scatter_dimension=1, tiled=True
        ).astype(jnp.float32),
        lax.psum_scatter(
            summed[1].astype(jnp.bfloat16), "dp", scatter_dimension=0, tiled=True
        ).astype(jnp.float32),
    )
    return (next_input, sent_back, expand_grad[None], reduce_grad[None], filter_grad[None])


VMEM_BYTES = 58 * 1024 * 1024


def interleave(table, order_count):
    rows = table.shape[0]
    return table.reshape(rows, 2, order_count).transpose(0, 2, 1).reshape(rows, 2 * order_count)


def recursion_kernel(cycles, main_ref, back_ref, start_ref, cos_ref, weight_ref, valid_ref,
                     analysis_ref, synthesis_ref, table_ref):
    order_count = start_ref.shape[0]
    slots = start_ref.shape[1]
    orders = valid_ref[...]
    start = start_ref[...]
    cosine = jnp.broadcast_to(cos_ref[...], (order_count, slots))
    previous = jnp.zeros_like(start)
    earlier = jnp.zeros_like(start)
    for degree in range(cycles):
        rising = main_ref[:, degree : degree + 1] * (
            cosine * previous - back_ref[:, degree : degree + 1] * earlier
        )
        current = jnp.where(
            orders == float(degree), start, jnp.where(orders < float(degree), rising, 0.0)
        )
        table_ref[:, degree, :] = current
        previous, earlier = current, previous
    weight = weight_ref[...]

    @pl.loop(0, order_count)
    def _(at):
        rows = table_ref[at]
        analysis_ref[at] = (rows * weight).astype(jnp.bfloat16)
        synthesis_ref[at] = rows.astype(jnp.bfloat16)


def legendre_tables(lat_index, order_index, cycles):
    lat_ok = (lat_index < cycles).astype(jnp.float32)
    order_ok = (order_index < cycles).astype(jnp.float32)
    colatitude = math.pi * (jnp.minimum(lat_index, cycles - 1).astype(jnp.float32) + 0.5) / cycles
    cosine = jnp.cos(colatitude)[None, :]
    sine_value = jnp.sin(colatitude)[None, :]
    order_value = jnp.minimum(order_index, cycles - 1).astype(jnp.float32)[:, None]
    log_start = 0.5 * (
        jnp.log((2.0 * order_value + 1.0) / (4.0 * math.pi))
        + lax.lgamma(2.0 * order_value + 1.0)
        - 2.0 * lax.lgamma(order_value + 1.0)
        - order_value * math.log(4.0)
    ) + order_value * jnp.log(sine_value)
    starting = jnp.exp(log_start) * (order_ok[:, None] * lat_ok[None, :])
    degree = jnp.arange(cycles, dtype=jnp.float32)[None, :]
    upper_term = jnp.maximum(4.0 * degree * degree - 1.0, 0.0)
    ratio_main = jnp.sqrt(
        upper_term / jnp.maximum(degree * degree - order_value * order_value, 1.0)
    )
    ratio_back = jnp.sqrt(
        jnp.maximum((degree - 1.0) ** 2 - order_value * order_value, 0.0)
        / jnp.maximum(4.0 * (degree - 1.0) ** 2 - 1.0, 1.0)
    )
    weight = cycle_weights(lat_index, cycles)[None, :]
    order_count, slots = starting.shape
    shape = (order_count, cycles, slots)
    return pl.pallas_call(
        functools.partial(recursion_kernel, cycles),
        out_shape=[jax.ShapeDtypeStruct(shape, jnp.bfloat16)] * 2,
        in_specs=[pl.BlockSpec(memory_space=pltpu.VMEM)] * 6,
        out_specs=[pl.BlockSpec(memory_space=pltpu.VMEM)] * 2,
        scratch_shapes=[pltpu.VMEM(shape, jnp.float32)],
        compiler_params=pltpu.CompilerParams(vmem_limit_bytes=24 * 1024 * 1024),
        cost_estimate=pl.CostEstimate(
            flops=12 * order_count * cycles * slots, bytes_accessed=20_000_000, transcendentals=0
        ),
        name="recursion",
    )(ratio_main, ratio_back, starting, cosine, weight, jnp.broadcast_to(order_value, (order_count, slots)))


def dot32(left, right):
    return jnp.dot(left, right, preferred_element_type=jnp.float32)


def turned_dot(left, right):
    return lax.dot_general(
        left, right, (((0,), (0,)), ((), ())), preferred_element_type=jnp.float32
    )


def value_kernel(cells, mask_ref, x_ref, own_ref, far_ref, inv_own_ref, inv_far_ref, expand_ref,
                 contract_ref, out_ref):
    base = pl.program_id(0) * cells
    for cell in range(cells):
        mixed = (
            x_ref[cell].astype(jnp.float32)
            + dot32(inv_own_ref[...], own_ref[cell])
            + dot32(inv_far_ref[...], far_ref[cell])
        )
        hidden = gelu_value(dot32(mixed.astype(jnp.bfloat16), expand_ref[...])).astype(jnp.bfloat16)
        result = mixed + dot32(hidden, contract_ref[...])
        out_ref[cell] = (result * mask_ref[base + cell]).astype(jnp.bfloat16)


def slope_kernel(cells, mask_ref, x_ref, grad_ref, own_ref, far_ref, inv_own_ref, inv_far_ref,
                 turn_own_ref, turn_far_ref, expand_ref, expand_t_ref, contract_t_ref,
                 mixed_out, own_out, far_out, sums_ref,
                 mixed_all, masked_all, hidden_all, pre_all):
    base = pl.program_id(0) * cells
    points = x_ref.shape[1]

    @pl.when(pl.program_id(0) == 0)
    def _():
        sums_ref[...] = jnp.zeros_like(sums_ref)

    for cell in range(cells):
        rows = pl.ds(cell * points, points)
        mixed = (
            x_ref[cell].astype(jnp.float32)
            + dot32(inv_own_ref[...], own_ref[cell])
            + dot32(inv_far_ref[...], far_ref[cell])
        )
        mixed_b = mixed.astype(jnp.bfloat16)
        mixed_all[rows, :] = mixed_b
        pre_act = dot32(mixed_b, expand_ref[...])
        both = 0.5 * (1.0 + lax.erf(pre_act * ROOT_HALF))
        hidden_all[rows, :] = (pre_act * both).astype(jnp.bfloat16)
        slope = both + pre_act * jnp.exp(-0.5 * pre_act * pre_act) * INV_ROOT_TAU
        masked = grad_ref[cell].astype(jnp.float32) * mask_ref[base + cell]
        masked_b = masked.astype(jnp.bfloat16)
        masked_all[rows, :] = masked_b
        grad_pre = (dot32(masked_b, contract_t_ref[...]) * slope).astype(jnp.bfloat16)
        pre_all[rows, :] = grad_pre
        grad_mixed = (masked + dot32(grad_pre, expand_t_ref[...])).astype(jnp.bfloat16)
        mixed_out[cell] = grad_mixed
        own_out[cell] = dot32(turn_own_ref[...], grad_mixed).astype(jnp.bfloat16)
        far_out[cell] = dot32(turn_far_ref[...], grad_mixed).astype(jnp.bfloat16)
    sums_ref[0] += turned_dot(mixed_all[...], pre_all[...])
    sums_ref[1] += turned_dot(masked_all[...], hidden_all[...])


def row_spec(cells, array):
    return pl.BlockSpec((cells,) + array.shape[1:], lambda at: (at,) + (0,) * (array.ndim - 1))


def whole_spec(array):
    return pl.BlockSpec(array.shape, lambda at: (0,) * array.ndim)


def cells_at_once(row_count, most):
    return max(c for c in range(1, most + 1) if row_count % c == 0)


def value_rows(mask, x, own, far, inv_own, inv_far, expand, contract):
    cells = cells_at_once(x.shape[0], 2)
    work = 4 * x.shape[0] * x.shape[1] * expand.size
    return pl.pallas_call(
        functools.partial(value_kernel, cells),
        grid=(x.shape[0] // cells,),
        out_shape=jax.ShapeDtypeStruct(x.shape, jnp.bfloat16),
        in_specs=[pl.BlockSpec(memory_space=pltpu.SMEM)]
        + [row_spec(cells, a) for a in (x, own, far)]
        + [whole_spec(a) for a in (inv_own, inv_far, expand, contract)],
        out_specs=row_spec(cells, x),
        compiler_params=pltpu.CompilerParams(vmem_limit_bytes=VMEM_BYTES),
        cost_estimate=pl.CostEstimate(flops=5 * work, bytes_accessed=8 * x.size, transcendentals=0),
        name="value_rows",
    )(mask, x, own, far, inv_own, inv_far, expand, contract)


def slope_rows(mask, x, grad, own, far, inv_own, inv_far, expand, contract):
    cells = cells_at_once(x.shape[0], 2)
    points, chan = x.shape[1:]
    hid = expand.shape[1]
    work = 10 * x.shape[0] * points * expand.size
    rows = [x, grad, own, far]
    whole = [inv_own, inv_far, inv_own.T, inv_far.T, expand, expand.T, contract.T]
    sums = jax.ShapeDtypeStruct((2, chan, hid), jnp.float32)
    return pl.pallas_call(
        functools.partial(slope_kernel, cells),
        grid=(x.shape[0] // cells,),
        out_shape=[jax.ShapeDtypeStruct(a.shape, jnp.bfloat16) for a in (x, own, far)] + [sums],
        in_specs=[pl.BlockSpec(memory_space=pltpu.SMEM)]
        + [row_spec(cells, a) for a in rows]
        + [whole_spec(a) for a in whole],
        out_specs=[row_spec(cells, a) for a in (x, own, far)] + [whole_spec(sums)],
        scratch_shapes=[
            pltpu.VMEM((cells * points, chan), jnp.bfloat16),
            pltpu.VMEM((cells * points, chan), jnp.bfloat16),
            pltpu.VMEM((cells * points, hid), jnp.bfloat16),
            pltpu.VMEM((cells * points, hid), jnp.bfloat16),
        ],
        compiler_params=pltpu.CompilerParams(vmem_limit_bytes=VMEM_BYTES),
        cost_estimate=pl.CostEstimate(flops=4 * work, bytes_accessed=12 * x.size, transcendentals=0),
        name="slope_rows",
    )(mask, *rows, *whole)


def swap(block, axis, mask=1):
    return lax.ppermute(block, axis, [(i, i ^ mask) for i in range(lax.axis_size(axis))])


def pair_sum(block, axis):
    mask = 1
    while mask < lax.axis_size(axis):
        block = block + swap(block, axis, mask)
        mask *= 2
    return block


def scatter_sum(block, axis):
    mask = lax.axis_size(axis) // 2
    place = lax.axis_index(axis)
    while mask:
        low, high = jnp.split(block, 2, axis=-1)
        upper = (place & mask) != 0
        kept = jnp.where(upper, high, low).astype(jnp.float32)
        sent = jnp.where(upper, low, high).astype(jnp.bfloat16)
        block = kept + swap(sent, axis, mask).astype(jnp.float32)
        mask //= 2
    return block


def paired_on_device(
    fresh_input, saved_input, output_grad, expand_weight, reduce_weight, filter_weight, cycle_table
):
    slot_count = fresh_input.shape[2]
    position = lax.axis_index("sp")
    order_table = jnp.arange(slot_count * 2, dtype=jnp.int32)
    here, there = position * slot_count, (1 - position) * slot_count
    cut = functools.partial(lax.dynamic_slice_in_dim, slice_size=slot_count)
    own_cycles, far_cycles = cut(cycle_table, here), cut(cycle_table, there)
    own_orders, far_orders = cut(order_table, here), cut(order_table, there)
    cycle_mask = (own_cycles < NLAT).astype(jnp.float32)
    forward_own, inverse_own = fourier_tables(own_orders, NLAT, NLON)
    forward_far, inverse_far = fourier_tables(far_orders, NLAT, NLON)
    forward_own = interleave(forward_own, slot_count)
    forward_far = interleave(forward_far, slot_count)
    inverse_own = interleave(inverse_own.T, slot_count)
    inverse_far = interleave(inverse_far.T, slot_count)
    filt = filter_weight[0]
    expand = expand_weight[0]
    contract = reduce_weight[0]
    fresh = fresh_input[0, 0]
    saved = saved_input[0, 0]
    points, chan_count = fresh.shape[1:]

    def longitude(x, table):
        return jnp.einsum(
            "jnc,nk->jkc", x, table, preferred_element_type=jnp.float32
        ).astype(jnp.bfloat16)

    saved_far = swap(longitude(saved, forward_far), "sp")
    saved_own = longitude(saved, forward_own)
    fresh_send = longitude(fresh, forward_far)
    fresh_own = longitude(fresh, forward_own)
    analysis, synthesis = legendre_tables(
        jnp.concatenate([own_cycles, far_cycles]), own_orders, NLAT
    )

    def to_degrees(own, far, table):
        both = jnp.concatenate([own, far], axis=0)
        both = both.reshape(2 * slot_count, slot_count, 2, chan_count)
        return jnp.einsum("tlj,jtrc->trlc", table, both, preferred_element_type=jnp.float32)

    def to_rows(spectra, table):
        rows = jnp.einsum(
            "tlj,trlc->jtrc", table, spectra, preferred_element_type=jnp.float32
        ).astype(jnp.bfloat16)
        rows = rows.reshape(2 * slot_count, 2 * slot_count, chan_count)
        return rows[:slot_count], rows[slot_count:]

    def filtered(spectra):
        real_part = filt[0] * spectra[:, 0] - filt[1] * spectra[:, 1]
        imag_part = filt[0] * spectra[:, 1] + filt[1] * spectra[:, 0]
        return jnp.stack([real_part, imag_part], axis=1).astype(jnp.bfloat16)

    spectra = to_degrees(saved_own, saved_far, analysis)
    own_values, far_values = to_rows(filtered(spectra), synthesis)
    came_values = swap(far_values, "sp")
    fresh_far = swap(fresh_send, "sp")
    fresh_filtered = filtered(to_degrees(fresh_own, fresh_far, analysis))
    fresh_own_values, fresh_far_values = to_rows(fresh_filtered, synthesis)
    fresh_came = swap(fresh_far_values, "sp")

    grad_mixed, grad_own, grad_send, sums = slope_rows(
        cycle_mask, saved, output_grad[0, 0], own_values, came_values, inverse_own, inverse_far,
        expand, contract,
    )
    grad_far = swap(grad_send, "sp")
    block = value_rows(
        cycle_mask, fresh, fresh_own_values, fresh_came, inverse_own, inverse_far, expand, contract
    )
    next_input = from_behind(block[None, None], "pipe", 1)
    grad_filtered = to_degrees(grad_own, grad_far, synthesis)
    filter_real = jnp.sum(
        grad_filtered[:, 0] * spectra[:, 0] + grad_filtered[:, 1] * spectra[:, 1], axis=0
    )
    filter_imag = jnp.sum(
        grad_filtered[:, 1] * spectra[:, 0] - grad_filtered[:, 0] * spectra[:, 1], axis=0
    )
    grad_spectra = jnp.stack(
        [
            filt[0] * grad_filtered[:, 0] + filt[1] * grad_filtered[:, 1],
            filt[0] * grad_filtered[:, 1] - filt[1] * grad_filtered[:, 0],
        ],
        axis=1,
    ).astype(jnp.bfloat16)
    own_coeffs, far_coeffs = to_rows(grad_spectra, analysis)
    came_coeffs = swap(far_coeffs, "sp")
    filter_grad = pair_sum(pair_sum(jnp.stack([filter_real, filter_imag]), "sp"), "dp")
    sums = sums + swap(sums.astype(jnp.bfloat16), "sp").astype(jnp.float32)
    sums = scatter_sum(sums, "dp")
    grad_tokens = jnp.einsum(
        "jkc,nk->jnc", own_coeffs, forward_own, preferred_element_type=jnp.float32
    ) + jnp.einsum("jkc,nk->jnc", came_coeffs, forward_far, preferred_element_type=jnp.float32)
    input_grad = (
        (grad_mixed.astype(jnp.float32) + grad_tokens) * cycle_mask[:, None, None]
    ).astype(jnp.bfloat16)
    sent_back = from_behind(input_grad[None, None], "pipe", -1)
    return (next_input, sent_back, sums[0][None], sums[1].T[None], filter_grad[None])


def solution(mesh):
    groups = mesh.shape["dp"]
    paired = mesh.shape["sp"] == 2 and groups & (groups - 1) == 0
    return jax.shard_map(
        paired_on_device if paired else on_device,
        mesh=mesh,
        in_specs=(
            P("pipe", "dp", "sp", None, None),
            P("pipe", "dp", "sp", None, None),
            P("pipe", "dp", "sp", None, None),
            P("pipe", None, None),
            P("pipe", None, None),
            P("pipe", None, None, None),
            P(),
        ),
        out_specs=(
            P("pipe", "dp", "sp", None, None),
            P("pipe", "dp", "sp", None, None),
            P("pipe", None, "dp"),
            P("pipe", "dp", None),
            P("pipe", None, None, None),
        ),
        check_vma=False,
    )
```

```python
import functools
import math

import jax
import jax.numpy as jnp
from jax import lax
from jax.experimental import pallas as pl
from jax.experimental.pallas import tpu as pltpu
from jax.sharding import PartitionSpec as P

NLAT = 120
NLON = 240


ROOT_HALF = 0.7071067811865476
INV_ROOT_TAU = 0.3989422804014327


def from_behind(block, axis, distance):
    devices = range(lax.axis_size(axis))
    route = [(i - distance, i) for i in devices if i - distance in devices]
    return lax.ppermute(block, axis, route)


def gelu_value(pre_act):
    return 0.5 * pre_act * (1.0 + lax.erf(pre_act * ROOT_HALF))


def gelu_slope(pre_act):
    return (
        0.5 * (1.0 + lax.erf(pre_act * ROOT_HALF))
        + pre_act * jnp.exp(-0.5 * pre_act * pre_act) * INV_ROOT_TAU
    )


def legendre(lat_index, order_index, cycles):
    lat_ok = (lat_index < cycles).astype(jnp.float32)
    order_ok = (order_index < cycles).astype(jnp.float32)
    colatitude = math.pi * (jnp.minimum(lat_index, cycles - 1).astype(jnp.float32) + 0.5) / cycles
    cosine = jnp.cos(colatitude)[None, :]
    sine_value = jnp.sin(colatitude)[None, :]
    order_value = jnp.minimum(order_index, cycles - 1).astype(jnp.float32)[:, None]
    log_start = 0.5 * (
        jnp.log((2.0 * order_value + 1.0) / (4.0 * math.pi))
        + lax.lgamma(2.0 * order_value + 1.0)
        - 2.0 * lax.lgamma(order_value + 1.0)
        - order_value * math.log(4.0)
    ) + order_value * jnp.log(sine_value)
    starting = jnp.exp(log_start)
    zero_rows = jnp.zeros_like(starting)

    def advance(state_pair, degree):
        previous, earlier = state_pair
        degree_value = degree.astype(jnp.float32)
        upper_term = jnp.maximum(4.0 * degree_value * degree_value - 1.0, 0.0)
        ratio_main = jnp.sqrt(
            upper_term / jnp.maximum(degree_value * degree_value - order_value * order_value, 1.0)
        )
        ratio_back = jnp.sqrt(
            jnp.maximum((degree_value - 1.0) ** 2 - order_value * order_value, 0.0)
            / jnp.maximum(4.0 * (degree_value - 1.0) ** 2 - 1.0, 1.0)
        )
        rising = ratio_main * (cosine * previous - ratio_back * earlier)
        current = jnp.where(
            degree_value == order_value,
            starting,
            jnp.where(degree_value > order_value, rising, 0.0),
        )
        return ((current, previous), current)

    _, stacked = lax.scan(advance, (zero_rows, zero_rows), jnp.arange(cycles, dtype=jnp.int32))
    valid_mask = order_ok[:, None] * lat_ok[None, :]
    return jnp.transpose(stacked, (1, 0, 2)) * valid_mask[:, None, :]


def cycle_weights(lat_index, cycles):
    valid_cycle = (lat_index < cycles).astype(jnp.float32)
    colatitude = math.pi * (jnp.minimum(lat_index, cycles - 1).astype(jnp.float32) + 0.5) / cycles
    return math.pi / cycles * jnp.sin(colatitude) * valid_cycle


def fourier_tables(order_index, cycles, points):
    valid_order = (order_index < cycles).astype(jnp.float32)[None, :]
    order_value = jnp.minimum(order_index, cycles - 1)
    longitude = jnp.arange(points, dtype=jnp.int32)
    phase_angle = (
        2.0
        * math.pi
        / points
        * (longitude[:, None] * order_value[None, :] % points).astype(jnp.float32)
    )
    scaled = valid_order * (2.0 * math.pi / points)
    forward = jnp.concatenate(
        [jnp.cos(phase_angle) * scaled, -jnp.sin(phase_angle) * scaled], axis=1
    )
    order_scale = jnp.where(order_value == 0, 1.0, 2.0)[None, :] * valid_order / (2.0 * math.pi)
    inverse = jnp.concatenate(
        [jnp.cos(phase_angle) * order_scale, -jnp.sin(phase_angle) * order_scale], axis=1
    ).T
    return (forward.astype(jnp.bfloat16), inverse.astype(jnp.bfloat16))


def joint_orders(coeffs):
    return lax.all_to_all(coeffs, "sp", split_axis=3, concat_axis=1, tiled=True)


def joint_cycles(values):
    return lax.all_to_all(values, "sp", split_axis=1, concat_axis=3, tiled=True)


def spectral_pass(tokens, filt, forward, analysis, synthesis, inverse, to_orders, to_cycles):
    batch_count, row_count, points, chan_count = tokens.shape
    order_count = forward.shape[1] // 2
    coeffs = jnp.einsum(
        "sjnc,nk->sjkc", tokens, forward, preferred_element_type=jnp.float32
    ).astype(jnp.bfloat16)
    coeffs = coeffs.reshape(batch_count, row_count, 2, order_count, chan_count)
    arrived = to_orders(coeffs)
    spectra = jnp.einsum("tlj,sjrtc->strlc", analysis, arrived, preferred_element_type=jnp.float32)
    real_part = filt[0] * spectra[:, :, 0] - filt[1] * spectra[:, :, 1]
    imag_part = filt[0] * spectra[:, :, 1] + filt[1] * spectra[:, :, 0]
    filtered = jnp.stack([real_part, imag_part], axis=2).astype(jnp.bfloat16)
    values = jnp.einsum(
        "tlj,strlc->sjrtc", synthesis, filtered, preferred_element_type=jnp.float32
    ).astype(jnp.bfloat16)
    returned = to_cycles(values).reshape(batch_count, row_count, 2 * order_count, chan_count)
    spatial = jnp.einsum("sjkc,kn->sjnc", returned, inverse, preferred_element_type=jnp.float32)
    return (spatial, spectra)


def mlp_pass(tokens, spatial, expand, contract, cycle_mask):
    grid_shape = tokens.shape
    flat_rows = (tokens.astype(jnp.float32) + spatial).reshape(-1, grid_shape[-1])
    mixed_b = flat_rows.astype(jnp.bfloat16)
    hidden_pre = jnp.dot(mixed_b, expand, preferred_element_type=jnp.float32)
    hidden = gelu_value(hidden_pre).astype(jnp.bfloat16)
    result = flat_rows + jnp.dot(hidden, contract, preferred_element_type=jnp.float32)
    result = (result.reshape(grid_shape) * cycle_mask[:, None, None]).astype(jnp.bfloat16)
    return (result, mixed_b, hidden_pre, hidden)


def backward_rows(cotangent, cycle_mask, mixed_b, hidden_pre, hidden, expand, contract):
    chan_count = cotangent.shape[-1]
    masked = (cotangent * cycle_mask.astype(jnp.bfloat16)[:, None, None]).reshape(-1, chan_count)
    grad_reduce = jnp.dot(hidden.T, masked, preferred_element_type=jnp.float32)
    grad_hidden = jnp.dot(masked, contract.T, preferred_element_type=jnp.float32)
    grad_pre = (grad_hidden * gelu_slope(hidden_pre)).astype(jnp.bfloat16)
    grad_expand = jnp.dot(mixed_b.T, grad_pre, preferred_element_type=jnp.float32)
    grad_mixed = masked.astype(jnp.float32) + jnp.dot(
        grad_pre, expand.T, preferred_element_type=jnp.float32
    )
    return (grad_mixed, grad_expand, grad_reduce)


def on_device(
    fresh_input, saved_input, output_grad, expand_weight, reduce_weight, filter_weight, cycle_table
):
    slot_count = fresh_input.shape[2]
    position = lax.axis_index("sp")
    order_table = jnp.arange(slot_count * lax.axis_size("sp"), dtype=jnp.int32)
    own_cycles = lax.dynamic_slice_in_dim(cycle_table, position * slot_count, slot_count)
    own_orders = lax.dynamic_slice_in_dim(order_table, position * slot_count, slot_count)
    cycle_mask = (own_cycles < NLAT).astype(jnp.float32)
    table = legendre(cycle_table, own_orders, NLAT)
    analysis = (table * cycle_weights(cycle_table, NLAT)[None, None, :]).astype(jnp.bfloat16)
    synthesis = table.astype(jnp.bfloat16)
    forward, inverse = fourier_tables(order_table, NLAT, NLON)
    filt = filter_weight[0]
    expand = expand_weight[0]
    contract = reduce_weight[0]
    fresh = fresh_input[0, 0]
    saved = saved_input[0, 0]
    spatial, spectra = spectral_pass(
        jnp.stack([fresh, saved]),
        filt,
        forward,
        analysis,
        synthesis,
        inverse,
        joint_orders,
        joint_cycles,
    )
    fresh_spatial = spatial[0]
    saved_spatial = spatial[1]
    saved_spectra = spectra[1]
    block = mlp_pass(fresh, fresh_spatial, expand, contract, cycle_mask)[0]
    next_input = from_behind(block[None, None], "pipe", 1)
    _, mixed_b, hidden_pre, hidden = mlp_pass(saved, saved_spatial, expand, contract, cycle_mask)
    grad_mixed, grad_expand, grad_reduce = backward_rows(
        output_grad[0, 0], cycle_mask, mixed_b, hidden_pre, hidden, expand, contract
    )
    grid_shape = saved.shape
    row_count, points, chan_count = grid_shape
    order_count = forward.shape[1] // 2
    grad_rows = grad_mixed.reshape(grid_shape).astype(jnp.bfloat16)
    grad_values = jnp.einsum(
        "jnc,kn->jkc", grad_rows, inverse, preferred_element_type=jnp.float32
    ).astype(jnp.bfloat16)
    grad_values = grad_values.reshape(row_count, 2, order_count, chan_count)
    arrived = lax.all_to_all(grad_values, "sp", split_axis=2, concat_axis=0, tiled=True)
    grad_filtered = jnp.einsum(
        "tlj,jrtc->trlc", synthesis, arrived, preferred_element_type=jnp.float32
    )
    filter_real = jnp.sum(
        grad_filtered[:, 0] * saved_spectra[:, 0] + grad_filtered[:, 1] * saved_spectra[:, 1],
        axis=0,
    )
    filter_imag = jnp.sum(
        grad_filtered[:, 1] * saved_spectra[:, 0] - grad_filtered[:, 0] * saved_spectra[:, 1],
        axis=0,
    )
    grad_spectra = jnp.stack(
        [
            filt[0] * grad_filtered[:, 0] + filt[1] * grad_filtered[:, 1],
            filt[0] * grad_filtered[:, 1] - filt[1] * grad_filtered[:, 0],
        ],
        axis=1,
    ).astype(jnp.bfloat16)
    grad_coeffs = jnp.einsum(
        "tlj,trlc->jrtc", analysis, grad_spectra, preferred_element_type=jnp.float32
    ).astype(jnp.bfloat16)
    returned = lax.all_to_all(grad_coeffs, "sp", split_axis=0, concat_axis=2, tiled=True)
    grad_tokens = jnp.einsum(
        "jkc,nk->jnc",
        returned.reshape(row_count, 2 * order_count, chan_count),
        forward,
        preferred_element_type=jnp.float32,
    )
    input_grad = (
        (grad_mixed.reshape(grid_shape) + grad_tokens) * cycle_mask[:, None, None]
    ).astype(jnp.bfloat16)
    sent_back = from_behind(input_grad[None, None], "pipe", -1)
    filter_grad = lax.psum(jnp.stack([filter_real, filter_imag]), ("sp", "dp"))
    summed = (
        lax.psum(grad_expand.astype(jnp.bfloat16), "sp").astype(jnp.float32),
        lax.psum(grad_reduce.astype(jnp.bfloat16), "sp").astype(jnp.float32),
    )
    expand_grad, reduce_grad = (
        lax.psum_scatter(
            summed[0].astype(jnp.bfloat16), "dp", scatter_dimension=1, tiled=True
        ).astype(jnp.float32),
        lax.psum_scatter(
            summed[1].astype(jnp.bfloat16), "dp", scatter_dimension=0, tiled=True
        ).astype(jnp.float32),
    )
    return (next_input, sent_back, expand_grad[None], reduce_grad[None], filter_grad[None])


VMEM_BYTES = 58 * 1024 * 1024


def interleave(table, order_count):
    rows = table.shape[0]
    return table.reshape(rows, 2, order_count).transpose(0, 2, 1).reshape(rows, 2 * order_count)


def recursion_kernel(cycles, main_ref, back_ref, start_ref, cos_ref, weight_ref, valid_ref,
                     analysis_ref, synthesis_ref, table_ref):
    order_count = start_ref.shape[0]
    slots = start_ref.shape[1]
    orders = valid_ref[...]
    start = start_ref[...]
    cosine = jnp.broadcast_to(cos_ref[...], (order_count, slots))
    previous = jnp.zeros_like(start)
    earlier = jnp.zeros_like(start)
    for degree in range(cycles):
        rising = main_ref[:, degree : degree + 1] * (
            cosine * previous - back_ref[:, degree : degree + 1] * earlier
        )
        current = jnp.where(
            orders == float(degree), start, jnp.where(orders < float(degree), rising, 0.0)
        )
        table_ref[:, degree, :] = current
        previous, earlier = current, previous
    weight = weight_ref[...]

    @pl.loop(0, order_count)
    def _(at):
        rows = table_ref[at]
        analysis_ref[at] = (rows * weight).astype(jnp.bfloat16)
        synthesis_ref[at] = rows.astype(jnp.bfloat16)


def legendre_tables(lat_index, order_index, cycles):
    lat_ok = (lat_index < cycles).astype(jnp.float32)
    order_ok = (order_index < cycles).astype(jnp.float32)
    colatitude = math.pi * (jnp.minimum(lat_index, cycles - 1).astype(jnp.float32) + 0.5) / cycles
    cosine = jnp.cos(colatitude)[None, :]
    sine_value = jnp.sin(colatitude)[None, :]
    order_value = jnp.minimum(order_index, cycles - 1).astype(jnp.float32)[:, None]
    log_start = 0.5 * (
        jnp.log((2.0 * order_value + 1.0) / (4.0 * math.pi))
        + lax.lgamma(2.0 * order_value + 1.0)
        - 2.0 * lax.lgamma(order_value + 1.0)
        - order_value * math.log(4.0)
    ) + order_value * jnp.log(sine_value)
    starting = jnp.exp(log_start) * (order_ok[:, None] * lat_ok[None, :])
    degree = jnp.arange(cycles, dtype=jnp.float32)[None, :]
    upper_term = jnp.maximum(4.0 * degree * degree - 1.0, 0.0)
    ratio_main = jnp.sqrt(
        upper_term / jnp.maximum(degree * degree - order_value * order_value, 1.0)
    )
    ratio_back = jnp.sqrt(
        jnp.maximum((degree - 1.0) ** 2 - order_value * order_value, 0.0)
        / jnp.maximum(4.0 * (degree - 1.0) ** 2 - 1.0, 1.0)
    )
    weight = cycle_weights(lat_index, cycles)[None, :]
    order_count, slots = starting.shape
    shape = (order_count, cycles, slots)
    return pl.pallas_call(
        functools.partial(recursion_kernel, cycles),
        out_shape=[jax.ShapeDtypeStruct(shape, jnp.bfloat16)] * 2,
        in_specs=[pl.BlockSpec(memory_space=pltpu.VMEM)] * 6,
        out_specs=[pl.BlockSpec(memory_space=pltpu.VMEM)] * 2,
        scratch_shapes=[pltpu.VMEM(shape, jnp.float32)],
        compiler_params=pltpu.CompilerParams(vmem_limit_bytes=24 * 1024 * 1024),
        cost_estimate=pl.CostEstimate(
            flops=12 * order_count * cycles * slots, bytes_accessed=20_000_000, transcendentals=0
        ),
        name="recursion",
    )(ratio_main, ratio_back, starting, cosine, weight, jnp.broadcast_to(order_value, (order_count, slots)))


def dot32(left, right):
    return jnp.dot(left, right, preferred_element_type=jnp.float32)


def turned_dot(left, right):
    return lax.dot_general(
        left, right, (((0,), (0,)), ((), ())), preferred_element_type=jnp.float32
    )


def value_kernel(cells, first, mask_ref, x_ref, own_ref, far_ref, inv_own_ref, inv_far_ref, expand_ref,
                 contract_ref, out_ref):
    base = first + pl.program_id(0) * cells
    for cell in range(cells):
        mixed = (
            x_ref[cell].astype(jnp.float32)
            + dot32(inv_own_ref[...], own_ref[cell])
            + dot32(inv_far_ref[...], far_ref[cell])
        )
        hidden = gelu_value(dot32(mixed.astype(jnp.bfloat16), expand_ref[...])).astype(jnp.bfloat16)
        result = mixed + dot32(hidden, contract_ref[...])
        out_ref[cell] = (result * mask_ref[base + cell]).astype(jnp.bfloat16)


def slope_kernel(cells, first, mask_ref, x_ref, grad_ref, own_ref, far_ref, inv_own_ref, inv_far_ref,
                 turn_own_ref, turn_far_ref, expand_ref, expand_t_ref, contract_t_ref,
                 mixed_out, own_out, far_out, sums_ref,
                 mixed_all, masked_all, hidden_all, pre_all):
    base = first + pl.program_id(0) * cells
    points = x_ref.shape[1]

    @pl.when(pl.program_id(0) == 0)
    def _():
        sums_ref[...] = jnp.zeros_like(sums_ref)

    for cell in range(cells):
        rows = pl.ds(cell * points, points)
        mixed = (
            x_ref[cell].astype(jnp.float32)
            + dot32(inv_own_ref[...], own_ref[cell])
            + dot32(inv_far_ref[...], far_ref[cell])
        )
        mixed_b = mixed.astype(jnp.bfloat16)
        mixed_all[rows, :] = mixed_b
        pre_act = dot32(mixed_b, expand_ref[...])
        both = 0.5 * (1.0 + lax.erf(pre_act * ROOT_HALF))
        hidden_all[rows, :] = (pre_act * both).astype(jnp.bfloat16)
        slope = both + pre_act * jnp.exp(-0.5 * pre_act * pre_act) * INV_ROOT_TAU
        masked = grad_ref[cell].astype(jnp.float32) * mask_ref[base + cell]
        masked_b = masked.astype(jnp.bfloat16)
        masked_all[rows, :] = masked_b
        grad_pre = (dot32(masked_b, contract_t_ref[...]) * slope).astype(jnp.bfloat16)
        pre_all[rows, :] = grad_pre
        grad_mixed = (masked + dot32(grad_pre, expand_t_ref[...])).astype(jnp.bfloat16)
        mixed_out[cell] = grad_mixed
        own_out[cell] = dot32(turn_own_ref[...], grad_mixed).astype(jnp.bfloat16)
        far_out[cell] = dot32(turn_far_ref[...], grad_mixed).astype(jnp.bfloat16)
    sums_ref[0] += turned_dot(mixed_all[...], pre_all[...])
    sums_ref[1] += turned_dot(masked_all[...], hidden_all[...])


def row_spec(cells, array, first=0):
    skip = first // cells
    return pl.BlockSpec(
        (cells,) + array.shape[1:], lambda at: (at + skip,) + (0,) * (array.ndim - 1)
    )


def whole_spec(array):
    return pl.BlockSpec(array.shape, lambda at: (0,) * array.ndim)


def cells_at_once(row_count, most):
    return max(c for c in range(1, most + 1) if row_count % c == 0)


def value_rows(mask, first, x, own, far, inv_own, inv_far, expand, contract):
    count = far.shape[0]
    cells = cells_at_once(math.gcd(count, first or count), 2)
    points, chan = x.shape[1:]
    out = jax.ShapeDtypeStruct((count, points, chan), jnp.bfloat16)
    work = 4 * count * points * expand.size
    return pl.pallas_call(
        functools.partial(value_kernel, cells, first),
        grid=(count // cells,),
        out_shape=out,
        in_specs=[pl.BlockSpec(memory_space=pltpu.SMEM), row_spec(cells, x, first)]
        + [row_spec(cells, a) for a in (own, far)]
        + [whole_spec(a) for a in (inv_own, inv_far, expand, contract)],
        out_specs=row_spec(cells, out),
        compiler_params=pltpu.CompilerParams(vmem_limit_bytes=VMEM_BYTES),
        cost_estimate=pl.CostEstimate(
            flops=2 * work, bytes_accessed=8 * count * points * chan, transcendentals=0
        ),
        name="value_rows",
    )(mask, x, own, far, inv_own, inv_far, expand, contract)


def slope_rows(mask, first, x, grad, own, far, inv_own, inv_far, expand, contract):
    count = far.shape[0]
    cells = cells_at_once(math.gcd(count, first or count), 2)
    points, chan = x.shape[1:]
    hid = expand.shape[1]
    out = jax.ShapeDtypeStruct((count, points, chan), jnp.bfloat16)
    work = 10 * count * points * expand.size
    whole = [inv_own, inv_far, inv_own.T, inv_far.T, expand, expand.T, contract.T]
    sums = jax.ShapeDtypeStruct((2, chan, hid), jnp.float32)
    return pl.pallas_call(
        functools.partial(slope_kernel, cells, first),
        grid=(count // cells,),
        out_shape=[out] + [jax.ShapeDtypeStruct(a.shape, jnp.bfloat16) for a in (own, far)] + [sums],
        in_specs=[pl.BlockSpec(memory_space=pltpu.SMEM)]
        + [row_spec(cells, a, first) for a in (x, grad)]
        + [row_spec(cells, a) for a in (own, far)]
        + [whole_spec(a) for a in whole],
        out_specs=[row_spec(cells, a) for a in (out, own, far)] + [whole_spec(sums)],
        scratch_shapes=[
            pltpu.VMEM((cells * points, chan), jnp.bfloat16),
            pltpu.VMEM((cells * points, chan), jnp.bfloat16),
            pltpu.VMEM((cells * points, hid), jnp.bfloat16),
            pltpu.VMEM((cells * points, hid), jnp.bfloat16),
        ],
        compiler_params=pltpu.CompilerParams(vmem_limit_bytes=VMEM_BYTES),
        cost_estimate=pl.CostEstimate(
            flops=2 * work, bytes_accessed=12 * count * points * chan, transcendentals=0
        ),
        name="slope_rows",
    )(mask, x, grad, own, far, *whole)


def swap(block, axis, mask=1):
    return lax.ppermute(block, axis, [(i, i ^ mask) for i in range(lax.axis_size(axis))])


def pair_sum(block, axis):
    mask = 1
    while mask < lax.axis_size(axis):
        block = block + swap(block, axis, mask)
        mask *= 2
    return block


def scatter_sum(block, axis):
    mask = lax.axis_size(axis) // 2
    place = lax.axis_index(axis)
    while mask:
        low, high = jnp.split(block, 2, axis=-1)
        upper = (place & mask) != 0
        kept = jnp.where(upper, high, low).astype(jnp.float32)
        sent = jnp.where(upper, low, high).astype(jnp.bfloat16)
        block = kept + swap(sent, axis, mask).astype(jnp.float32)
        mask //= 2
    return block


def paired_on_device(
    fresh_input, saved_input, output_grad, expand_weight, reduce_weight, filter_weight, cycle_table
):
    slot_count = fresh_input.shape[2]
    position = lax.axis_index("sp")
    order_table = jnp.arange(slot_count * 2, dtype=jnp.int32)
    here, there = position * slot_count, (1 - position) * slot_count
    cut = functools.partial(lax.dynamic_slice_in_dim, slice_size=slot_count)
    own_cycles, far_cycles = cut(cycle_table, here), cut(cycle_table, there)
    own_orders, far_orders = cut(order_table, here), cut(order_table, there)
    cycle_mask = (own_cycles < NLAT).astype(jnp.float32)
    forward_own, inverse_own = fourier_tables(own_orders, NLAT, NLON)
    forward_far, inverse_far = fourier_tables(far_orders, NLAT, NLON)
    forward_own = interleave(forward_own, slot_count)
    forward_far = interleave(forward_far, slot_count)
    inverse_own = interleave(inverse_own.T, slot_count)
    inverse_far = interleave(inverse_far.T, slot_count)
    filt = filter_weight[0]
    expand = expand_weight[0]
    contract = reduce_weight[0]
    fresh = fresh_input[0, 0]
    saved = saved_input[0, 0]
    points, chan_count = fresh.shape[1:]

    def longitude(x, table):
        return jnp.einsum(
            "jnc,nk->jkc", x, table, preferred_element_type=jnp.float32
        ).astype(jnp.bfloat16)

    half = slot_count // 2
    parts = ((0, half), (half, slot_count))

    def exchange(pieces):
        return [swap(piece, "sp") for piece in pieces]

    def after(values, *before):
        return lax.optimization_barrier((values,) + before)[0]

    saved_send = longitude(saved, forward_far)
    saved_far = swap(saved_send, "sp")
    saved_own = longitude(saved, forward_own)
    fresh_later = after(fresh, saved_own)
    fresh_send = longitude(fresh_later, forward_far)
    fresh_send = [fresh_send[low:high] for low, high in parts]
    fresh_far = [swap(after(fresh_send[0], saved_send), "sp")]
    fresh_own = longitude(fresh_later, forward_own)
    analysis, synthesis = legendre_tables(
        jnp.concatenate([own_cycles, far_cycles]), own_orders, NLAT
    )

    def to_degrees(pieces, table):
        both = jnp.concatenate(pieces, axis=0)
        both = both.reshape(2 * slot_count, slot_count, 2, chan_count)
        return jnp.einsum("tlj,jtrc->trlc", table, both, preferred_element_type=jnp.float32)

    def to_rows(spectra, table, low, high):
        rows = jnp.einsum(
            "tlj,trlc->jtrc", table[:, :, low:high], spectra, preferred_element_type=jnp.float32
        ).astype(jnp.bfloat16)
        return rows.reshape(high - low, 2 * slot_count, chan_count)

    def own_rows(spectra, table):
        return [to_rows(spectra, table, low, high) for low, high in parts]

    def far_rows(spectra, table):
        return [
            to_rows(spectra, table, slot_count + low, slot_count + high) for low, high in parts
        ]

    def filtered(spectra):
        real_part = filt[0] * spectra[:, 0] - filt[1] * spectra[:, 1]
        imag_part = filt[0] * spectra[:, 1] + filt[1] * spectra[:, 0]
        return jnp.stack([real_part, imag_part], axis=1).astype(jnp.bfloat16)

    spectra = to_degrees([saved_own, saved_far], analysis)
    saved_filtered = filtered(spectra)
    send_values = far_rows(saved_filtered, synthesis)
    send_values[1] = after(send_values[1], send_values[0])
    came_values = exchange(send_values)
    fresh_far.append(swap(after(fresh_send[1], send_values), "sp"))
    own_values = own_rows(after(saved_filtered, send_values), synthesis)

    slopes = []
    for (low, _), own, came in zip(parts, own_values, came_values):
        slopes.append(
            slope_rows(
                cycle_mask, low, saved, output_grad[0, 0], after(own, slopes), came, inverse_own,
                inverse_far, expand, contract,
            )
        )
    grad_mixed, grad_own, grad_send, sums = zip(*slopes)
    grad_far = exchange(grad_send)

    fresh_far = after(fresh_far, grad_send)
    fresh_filtered = filtered(to_degrees([fresh_own] + fresh_far, analysis))
    fresh_send_values = far_rows(fresh_filtered, synthesis)
    fresh_came = exchange(fresh_send_values)
    fresh_own_values = own_rows(fresh_filtered, synthesis)
    sums = scatter_sum(sums[0] + sums[1], "dp")
    scattered = sums
    sums = sums + swap(sums.astype(jnp.bfloat16), "sp").astype(jnp.float32)

    grad_far = after(list(grad_far), fresh_send_values)
    grad_filtered = to_degrees(list(grad_own) + grad_far, synthesis)
    filter_real = jnp.sum(
        grad_filtered[:, 0] * spectra[:, 0] + grad_filtered[:, 1] * spectra[:, 1], axis=0
    )
    filter_imag = jnp.sum(
        grad_filtered[:, 1] * spectra[:, 0] - grad_filtered[:, 0] * spectra[:, 1], axis=0
    )
    grad_spectra = jnp.stack(
        [
            filt[0] * grad_filtered[:, 0] + filt[1] * grad_filtered[:, 1],
            filt[0] * grad_filtered[:, 1] - filt[1] * grad_filtered[:, 0],
        ],
        axis=1,
    ).astype(jnp.bfloat16)
    send_coeffs = far_rows(after(grad_spectra, scattered), analysis)
    send_coeffs[1] = after(send_coeffs[1], send_coeffs[0])
    came_coeffs = exchange(send_coeffs)
    fresh_came = after(fresh_came, send_coeffs)
    own_coeffs = own_rows(after(grad_spectra, send_coeffs), analysis)
    filter_grad = pair_sum(jnp.stack([filter_real, filter_imag]), "dp")
    fresh_came[1] = after(fresh_came[1], filter_grad, sums)
    filter_grad = pair_sum(filter_grad, "sp")

    def joined(pieces):
        whole = jnp.zeros((1, 1) + fresh.shape, jnp.bfloat16)
        for (low, _), piece in zip(parts, pieces):
            whole = lax.dynamic_update_slice(whole, piece[None, None], (0, 0, low, 0, 0))
        return whole

    next_pieces, back_pieces = [], []
    for at, (low, high) in enumerate(parts):
        block = value_rows(
            cycle_mask, low, fresh, after(fresh_own_values[at], back_pieces), fresh_came[at],
            inverse_own, inverse_far, expand, contract,
        )
        next_pieces.append(block)
        grad_tokens = jnp.einsum(
            "jkc,nk->jnc", own_coeffs[at], forward_own, preferred_element_type=jnp.float32
        ) + jnp.einsum(
            "jkc,nk->jnc", came_coeffs[at], forward_far, preferred_element_type=jnp.float32
        )
        piece = (grad_mixed[at].astype(jnp.float32) + grad_tokens) * cycle_mask[low:high, None, None]
        back_pieces.append(piece.astype(jnp.bfloat16))
    next_pieces = [from_behind(piece, "pipe", 1) for piece in next_pieces]
    back_pieces = [from_behind(piece, "pipe", -1) for piece in back_pieces]
    return (
        joined(next_pieces),
        joined(back_pieces),
        sums[0][None],
        sums[1].T[None],
        filter_grad[None],
    )


def solution(mesh):
    groups = mesh.shape["dp"]
    paired = mesh.shape["sp"] == 2 and groups & (groups - 1) == 0
    return jax.shard_map(
        paired_on_device if paired else on_device,
        mesh=mesh,
        in_specs=(
            P("pipe", "dp", "sp", None, None),
            P("pipe", "dp", "sp", None, None),
            P("pipe", "dp", "sp", None, None),
            P("pipe", None, None),
            P("pipe", None, None),
            P("pipe", None, None, None),
            P(),
        ),
        out_specs=(
            P("pipe", "dp", "sp", None, None),
            P("pipe", "dp", "sp", None, None),
            P("pipe", None, "dp"),
            P("pipe", "dp", None),
            P("pipe", None, None, None),
        ),
        check_vma=False,
    )
```

```python
import functools
import math

import jax
import jax.numpy as jnp
from jax import lax
from jax.experimental import pallas as pl
from jax.experimental.pallas import tpu as pltpu
from jax.sharding import PartitionSpec as P

NLAT = 120
NLON = 240


ROOT_HALF = 0.7071067811865476
INV_ROOT_TAU = 0.3989422804014327


def from_behind(block, axis, distance):
    devices = range(lax.axis_size(axis))
    route = [(i - distance, i) for i in devices if i - distance in devices]
    return lax.ppermute(block, axis, route)


def gelu_value(pre_act):
    return 0.5 * pre_act * (1.0 + lax.erf(pre_act * ROOT_HALF))


def gelu_slope(pre_act):
    return (
        0.5 * (1.0 + lax.erf(pre_act * ROOT_HALF))
        + pre_act * jnp.exp(-0.5 * pre_act * pre_act) * INV_ROOT_TAU
    )


def legendre(lat_index, order_index, cycles):
    lat_ok = (lat_index < cycles).astype(jnp.float32)
    order_ok = (order_index < cycles).astype(jnp.float32)
    colatitude = math.pi * (jnp.minimum(lat_index, cycles - 1).astype(jnp.float32) + 0.5) / cycles
    cosine = jnp.cos(colatitude)[None, :]
    sine_value = jnp.sin(colatitude)[None, :]
    order_value = jnp.minimum(order_index, cycles - 1).astype(jnp.float32)[:, None]
    log_start = 0.5 * (
        jnp.log((2.0 * order_value + 1.0) / (4.0 * math.pi))
        + lax.lgamma(2.0 * order_value + 1.0)
        - 2.0 * lax.lgamma(order_value + 1.0)
        - order_value * math.log(4.0)
    ) + order_value * jnp.log(sine_value)
    starting = jnp.exp(log_start)
    zero_rows = jnp.zeros_like(starting)

    def advance(state_pair, degree):
        previous, earlier = state_pair
        degree_value = degree.astype(jnp.float32)
        upper_term = jnp.maximum(4.0 * degree_value * degree_value - 1.0, 0.0)
        ratio_main = jnp.sqrt(
            upper_term / jnp.maximum(degree_value * degree_value - order_value * order_value, 1.0)
        )
        ratio_back = jnp.sqrt(
            jnp.maximum((degree_value - 1.0) ** 2 - order_value * order_value, 0.0)
            / jnp.maximum(4.0 * (degree_value - 1.0) ** 2 - 1.0, 1.0)
        )
        rising = ratio_main * (cosine * previous - ratio_back * earlier)
        current = jnp.where(
            degree_value == order_value,
            starting,
            jnp.where(degree_value > order_value, rising, 0.0),
        )
        return ((current, previous), current)

    _, stacked = lax.scan(advance, (zero_rows, zero_rows), jnp.arange(cycles, dtype=jnp.int32))
    valid_mask = order_ok[:, None] * lat_ok[None, :]
    return jnp.transpose(stacked, (1, 0, 2)) * valid_mask[:, None, :]


def cycle_weights(lat_index, cycles):
    valid_cycle = (lat_index < cycles).astype(jnp.float32)
    colatitude = math.pi * (jnp.minimum(lat_index, cycles - 1).astype(jnp.float32) + 0.5) / cycles
    return math.pi / cycles * jnp.sin(colatitude) * valid_cycle


def fourier_tables(order_index, cycles, points):
    valid_order = (order_index < cycles).astype(jnp.float32)[None, :]
    order_value = jnp.minimum(order_index, cycles - 1)
    longitude = jnp.arange(points, dtype=jnp.int32)
    phase_angle = (
        2.0
        * math.pi
        / points
        * (longitude[:, None] * order_value[None, :] % points).astype(jnp.float32)
    )
    scaled = valid_order * (2.0 * math.pi / points)
    forward = jnp.concatenate(
        [jnp.cos(phase_angle) * scaled, -jnp.sin(phase_angle) * scaled], axis=1
    )
    order_scale = jnp.where(order_value == 0, 1.0, 2.0)[None, :] * valid_order / (2.0 * math.pi)
    inverse = jnp.concatenate(
        [jnp.cos(phase_angle) * order_scale, -jnp.sin(phase_angle) * order_scale], axis=1
    ).T
    return (forward.astype(jnp.bfloat16), inverse.astype(jnp.bfloat16))


def joint_orders(coeffs):
    return lax.all_to_all(coeffs, "sp", split_axis=3, concat_axis=1, tiled=True)


def joint_cycles(values):
    return lax.all_to_all(values, "sp", split_axis=1, concat_axis=3, tiled=True)


def spectral_pass(tokens, filt, forward, analysis, synthesis, inverse, to_orders, to_cycles):
    batch_count, row_count, points, chan_count = tokens.shape
    order_count = forward.shape[1] // 2
    coeffs = jnp.einsum(
        "sjnc,nk->sjkc", tokens, forward, preferred_element_type=jnp.float32
    ).astype(jnp.bfloat16)
    coeffs = coeffs.reshape(batch_count, row_count, 2, order_count, chan_count)
    arrived = to_orders(coeffs)
    spectra = jnp.einsum("tlj,sjrtc->strlc", analysis, arrived, preferred_element_type=jnp.float32)
    real_part = filt[0] * spectra[:, :, 0] - filt[1] * spectra[:, :, 1]
    imag_part = filt[0] * spectra[:, :, 1] + filt[1] * spectra[:, :, 0]
    filtered = jnp.stack([real_part, imag_part], axis=2).astype(jnp.bfloat16)
    values = jnp.einsum(
        "tlj,strlc->sjrtc", synthesis, filtered, preferred_element_type=jnp.float32
    ).astype(jnp.bfloat16)
    returned = to_cycles(values).reshape(batch_count, row_count, 2 * order_count, chan_count)
    spatial = jnp.einsum("sjkc,kn->sjnc", returned, inverse, preferred_element_type=jnp.float32)
    return (spatial, spectra)


def mlp_pass(tokens, spatial, expand, contract, cycle_mask):
    grid_shape = tokens.shape
    flat_rows = (tokens.astype(jnp.float32) + spatial).reshape(-1, grid_shape[-1])
    mixed_b = flat_rows.astype(jnp.bfloat16)
    hidden_pre = jnp.dot(mixed_b, expand, preferred_element_type=jnp.float32)
    hidden = gelu_value(hidden_pre).astype(jnp.bfloat16)
    result = flat_rows + jnp.dot(hidden, contract, preferred_element_type=jnp.float32)
    result = (result.reshape(grid_shape) * cycle_mask[:, None, None]).astype(jnp.bfloat16)
    return (result, mixed_b, hidden_pre, hidden)


def backward_rows(cotangent, cycle_mask, mixed_b, hidden_pre, hidden, expand, contract):
    chan_count = cotangent.shape[-1]
    masked = (cotangent * cycle_mask.astype(jnp.bfloat16)[:, None, None]).reshape(-1, chan_count)
    grad_reduce = jnp.dot(hidden.T, masked, preferred_element_type=jnp.float32)
    grad_hidden = jnp.dot(masked, contract.T, preferred_element_type=jnp.float32)
    grad_pre = (grad_hidden * gelu_slope(hidden_pre)).astype(jnp.bfloat16)
    grad_expand = jnp.dot(mixed_b.T, grad_pre, preferred_element_type=jnp.float32)
    grad_mixed = masked.astype(jnp.float32) + jnp.dot(
        grad_pre, expand.T, preferred_element_type=jnp.float32
    )
    return (grad_mixed, grad_expand, grad_reduce)


def on_device(
    fresh_input, saved_input, output_grad, expand_weight, reduce_weight, filter_weight, cycle_table
):
    slot_count = fresh_input.shape[2]
    position = lax.axis_index("sp")
    order_table = jnp.arange(slot_count * lax.axis_size("sp"), dtype=jnp.int32)
    own_cycles = lax.dynamic_slice_in_dim(cycle_table, position * slot_count, slot_count)
    own_orders = lax.dynamic_slice_in_dim(order_table, position * slot_count, slot_count)
    cycle_mask = (own_cycles < NLAT).astype(jnp.float32)
    table = legendre(cycle_table, own_orders, NLAT)
    analysis = (table * cycle_weights(cycle_table, NLAT)[None, None, :]).astype(jnp.bfloat16)
    synthesis = table.astype(jnp.bfloat16)
    forward, inverse = fourier_tables(order_table, NLAT, NLON)
    filt = filter_weight[0]
    expand = expand_weight[0]
    contract = reduce_weight[0]
    fresh = fresh_input[0, 0]
    saved = saved_input[0, 0]
    spatial, spectra = spectral_pass(
        jnp.stack([fresh, saved]),
        filt,
        forward,
        analysis,
        synthesis,
        inverse,
        joint_orders,
        joint_cycles,
    )
    fresh_spatial = spatial[0]
    saved_spatial = spatial[1]
    saved_spectra = spectra[1]
    block = mlp_pass(fresh, fresh_spatial, expand, contract, cycle_mask)[0]
    next_input = from_behind(block[None, None], "pipe", 1)
    _, mixed_b, hidden_pre, hidden = mlp_pass(saved, saved_spatial, expand, contract, cycle_mask)
    grad_mixed, grad_expand, grad_reduce = backward_rows(
        output_grad[0, 0], cycle_mask, mixed_b, hidden_pre, hidden, expand, contract
    )
    grid_shape = saved.shape
    row_count, points, chan_count = grid_shape
    order_count = forward.shape[1] // 2
    grad_rows = grad_mixed.reshape(grid_shape).astype(jnp.bfloat16)
    grad_values = jnp.einsum(
        "jnc,kn->jkc", grad_rows, inverse, preferred_element_type=jnp.float32
    ).astype(jnp.bfloat16)
    grad_values = grad_values.reshape(row_count, 2, order_count, chan_count)
    arrived = lax.all_to_all(grad_values, "sp", split_axis=2, concat_axis=0, tiled=True)
    grad_filtered = jnp.einsum(
        "tlj,jrtc->trlc", synthesis, arrived, preferred_element_type=jnp.float32
    )
    filter_real = jnp.sum(
        grad_filtered[:, 0] * saved_spectra[:, 0] + grad_filtered[:, 1] * saved_spectra[:, 1],
        axis=0,
    )
    filter_imag = jnp.sum(
        grad_filtered[:, 1] * saved_spectra[:, 0] - grad_filtered[:, 0] * saved_spectra[:, 1],
        axis=0,
    )
    grad_spectra = jnp.stack(
        [
            filt[0] * grad_filtered[:, 0] + filt[1] * grad_filtered[:, 1],
            filt[0] * grad_filtered[:, 1] - filt[1] * grad_filtered[:, 0],
        ],
        axis=1,
    ).astype(jnp.bfloat16)
    grad_coeffs = jnp.einsum(
        "tlj,trlc->jrtc", analysis, grad_spectra, preferred_element_type=jnp.float32
    ).astype(jnp.bfloat16)
    returned = lax.all_to_all(grad_coeffs, "sp", split_axis=0, concat_axis=2, tiled=True)
    grad_tokens = jnp.einsum(
        "jkc,nk->jnc",
        returned.reshape(row_count, 2 * order_count, chan_count),
        forward,
        preferred_element_type=jnp.float32,
    )
    input_grad = (
        (grad_mixed.reshape(grid_shape) + grad_tokens) * cycle_mask[:, None, None]
    ).astype(jnp.bfloat16)
    sent_back = from_behind(input_grad[None, None], "pipe", -1)
    filter_grad = lax.psum(jnp.stack([filter_real, filter_imag]), ("sp", "dp"))
    summed = (
        lax.psum(grad_expand.astype(jnp.bfloat16), "sp").astype(jnp.float32),
        lax.psum(grad_reduce.astype(jnp.bfloat16), "sp").astype(jnp.float32),
    )
    expand_grad, reduce_grad = (
        lax.psum_scatter(
            summed[0].astype(jnp.bfloat16), "dp", scatter_dimension=1, tiled=True
        ).astype(jnp.float32),
        lax.psum_scatter(
            summed[1].astype(jnp.bfloat16), "dp", scatter_dimension=0, tiled=True
        ).astype(jnp.float32),
    )
    return (next_input, sent_back, expand_grad[None], reduce_grad[None], filter_grad[None])


VMEM_BYTES = 58 * 1024 * 1024


def interleave(table, order_count):
    rows = table.shape[0]
    return table.reshape(rows, 2, order_count).transpose(0, 2, 1).reshape(rows, 2 * order_count)


def recursion_kernel(cycles, main_ref, back_ref, start_ref, cos_ref, weight_ref, valid_ref,
                     analysis_ref, synthesis_ref, table_ref):
    order_count = start_ref.shape[0]
    slots = start_ref.shape[1]
    orders = valid_ref[...]
    start = start_ref[...]
    cosine = jnp.broadcast_to(cos_ref[...], (order_count, slots))
    previous = jnp.zeros_like(start)
    earlier = jnp.zeros_like(start)
    step = main_ref.shape[2]

    def advance(block, state_pair):
        previous, earlier = state_pair
        main, back = main_ref[block], back_ref[block]
        for at in range(step):
            degree = block * step + at
            rising = main[:, at : at + 1] * (cosine * previous - back[:, at : at + 1] * earlier)
            reached = degree.astype(jnp.float32)
            current = jnp.where(
                orders == reached, start, jnp.where(orders < reached, rising, 0.0)
            )
            table_ref[:, degree, :] = current
            previous, earlier = current, previous
        return previous, earlier

    lax.fori_loop(0, cycles // step, advance, (previous, earlier))
    weight = weight_ref[...]

    @pl.loop(0, order_count)
    def _(at):
        rows = table_ref[at]
        analysis_ref[at] = (rows * weight).astype(jnp.bfloat16)
        synthesis_ref[at] = rows.astype(jnp.bfloat16)


def legendre_tables(lat_index, order_index, cycles):
    lat_ok = (lat_index < cycles).astype(jnp.float32)
    order_ok = (order_index < cycles).astype(jnp.float32)
    colatitude = math.pi * (jnp.minimum(lat_index, cycles - 1).astype(jnp.float32) + 0.5) / cycles
    cosine = jnp.cos(colatitude)[None, :]
    sine_value = jnp.sin(colatitude)[None, :]
    order_value = jnp.minimum(order_index, cycles - 1).astype(jnp.float32)[:, None]
    log_start = 0.5 * (
        jnp.log((2.0 * order_value + 1.0) / (4.0 * math.pi))
        + lax.lgamma(2.0 * order_value + 1.0)
        - 2.0 * lax.lgamma(order_value + 1.0)
        - order_value * math.log(4.0)
    ) + order_value * jnp.log(sine_value)
    starting = jnp.exp(log_start) * (order_ok[:, None] * lat_ok[None, :])
    degree = jnp.arange(cycles, dtype=jnp.float32)[None, :]
    upper_term = jnp.maximum(4.0 * degree * degree - 1.0, 0.0)
    ratio_main = jnp.sqrt(
        upper_term / jnp.maximum(degree * degree - order_value * order_value, 1.0)
    )
    ratio_back = jnp.sqrt(
        jnp.maximum((degree - 1.0) ** 2 - order_value * order_value, 0.0)
        / jnp.maximum(4.0 * (degree - 1.0) ** 2 - 1.0, 1.0)
    )
    step = math.gcd(cycles, 8)
    ratio_main, ratio_back = (
        ratio.reshape(-1, cycles // step, step).transpose(1, 0, 2)
        for ratio in (ratio_main, ratio_back)
    )
    weight = cycle_weights(lat_index, cycles)[None, :]
    order_count, slots = starting.shape
    shape = (order_count, cycles, slots)
    return pl.pallas_call(
        functools.partial(recursion_kernel, cycles),
        out_shape=[jax.ShapeDtypeStruct(shape, jnp.bfloat16)] * 2,
        in_specs=[pl.BlockSpec(memory_space=pltpu.VMEM)] * 6,
        out_specs=[pl.BlockSpec(memory_space=pltpu.VMEM)] * 2,
        scratch_shapes=[pltpu.VMEM(shape, jnp.float32)],
        compiler_params=pltpu.CompilerParams(vmem_limit_bytes=24 * 1024 * 1024),
        cost_estimate=pl.CostEstimate(
            flops=12 * order_count * cycles * slots, bytes_accessed=20_000_000, transcendentals=0
        ),
        name="recursion",
    )(ratio_main, ratio_back, starting, cosine, weight, jnp.broadcast_to(order_value, (order_count, slots)))


def dot32(left, right):
    return jnp.dot(left, right, preferred_element_type=jnp.float32)


def turned_dot(left, right):
    return lax.dot_general(
        left, right, (((0,), (0,)), ((), ())), preferred_element_type=jnp.float32
    )


def value_kernel(cells, first, mask_ref, x_ref, own_ref, far_ref, inv_own_ref, inv_far_ref, expand_ref,
                 contract_ref, out_ref):
    base = first + pl.program_id(0) * cells
    for cell in range(cells):
        mixed = (
            x_ref[cell].astype(jnp.float32)
            + dot32(inv_own_ref[...], own_ref[cell])
            + dot32(inv_far_ref[...], far_ref[cell])
        )
        hidden = gelu_value(dot32(mixed.astype(jnp.bfloat16), expand_ref[...])).astype(jnp.bfloat16)
        result = mixed + dot32(hidden, contract_ref[...])
        out_ref[cell] = (result * mask_ref[base + cell]).astype(jnp.bfloat16)


def slope_kernel(cells, first, mask_ref, x_ref, grad_ref, own_ref, far_ref, inv_own_ref, inv_far_ref,
                 turn_own_ref, turn_far_ref, expand_ref, expand_t_ref, contract_t_ref,
                 mixed_out, own_out, far_out, sums_ref,
                 mixed_all, masked_all, hidden_all, pre_all):
    base = first + pl.program_id(0) * cells
    points = x_ref.shape[1]

    @pl.when(pl.program_id(0) == 0)
    def _():
        sums_ref[...] = jnp.zeros_like(sums_ref)

    for cell in range(cells):
        rows = pl.ds(cell * points, points)
        mixed = (
            x_ref[cell].astype(jnp.float32)
            + dot32(inv_own_ref[...], own_ref[cell])
            + dot32(inv_far_ref[...], far_ref[cell])
        )
        mixed_b = mixed.astype(jnp.bfloat16)
        mixed_all[rows, :] = mixed_b
        pre_act = dot32(mixed_b, expand_ref[...])
        both = 0.5 * (1.0 + lax.erf(pre_act * ROOT_HALF))
        hidden_all[rows, :] = (pre_act * both).astype(jnp.bfloat16)
        slope = both + pre_act * jnp.exp(-0.5 * pre_act * pre_act) * INV_ROOT_TAU
        masked = grad_ref[cell].astype(jnp.float32) * mask_ref[base + cell]
        masked_b = masked.astype(jnp.bfloat16)
        masked_all[rows, :] = masked_b
        grad_pre = (dot32(masked_b, contract_t_ref[...]) * slope).astype(jnp.bfloat16)
        pre_all[rows, :] = grad_pre
        grad_mixed = (masked + dot32(grad_pre, expand_t_ref[...])).astype(jnp.bfloat16)
        mixed_out[cell] = grad_mixed
        own_out[cell] = dot32(turn_own_ref[...], grad_mixed).astype(jnp.bfloat16)
        far_out[cell] = dot32(turn_far_ref[...], grad_mixed).astype(jnp.bfloat16)
    sums_ref[0] += turned_dot(mixed_all[...], pre_all[...])
    sums_ref[1] += turned_dot(masked_all[...], hidden_all[...])


def row_spec(cells, array, first=0):
    skip = first // cells
    return pl.BlockSpec(
        (cells,) + array.shape[1:], lambda at: (at + skip,) + (0,) * (array.ndim - 1)
    )


def whole_spec(array):
    return pl.BlockSpec(array.shape, lambda at: (0,) * array.ndim)


def cells_at_once(row_count, most):
    return max(c for c in range(1, most + 1) if row_count % c == 0)


def value_rows(mask, first, x, own, far, inv_own, inv_far, expand, contract):
    count = far.shape[0]
    cells = cells_at_once(math.gcd(count, first or count), 2)
    points, chan = x.shape[1:]
    out = jax.ShapeDtypeStruct((count, points, chan), jnp.bfloat16)
    work = 4 * count * points * expand.size
    return pl.pallas_call(
        functools.partial(value_kernel, cells, first),
        grid=(count // cells,),
        out_shape=out,
        in_specs=[pl.BlockSpec(memory_space=pltpu.SMEM), row_spec(cells, x, first)]
        + [row_spec(cells, own, first), row_spec(cells, far)]
        + [whole_spec(a) for a in (inv_own, inv_far, expand, contract)],
        out_specs=row_spec(cells, out),
        compiler_params=pltpu.CompilerParams(vmem_limit_bytes=VMEM_BYTES),
        cost_estimate=pl.CostEstimate(
            flops=2 * work, bytes_accessed=8 * count * points * chan, transcendentals=0
        ),
        name="value_rows",
    )(mask, x, own, far, inv_own, inv_far, expand, contract)


def slope_rows(mask, first, x, grad, own, far, inv_own, inv_far, expand, contract):
    count = far.shape[0]
    cells = cells_at_once(math.gcd(count, first or count), 2)
    points, chan = x.shape[1:]
    hid = expand.shape[1]
    out = jax.ShapeDtypeStruct((count, points, chan), jnp.bfloat16)
    work = 10 * count * points * expand.size
    whole = [inv_own, inv_far, inv_own.T, inv_far.T, expand, expand.T, contract.T]
    sums = jax.ShapeDtypeStruct((2, chan, hid), jnp.float32)
    return pl.pallas_call(
        functools.partial(slope_kernel, cells, first),
        grid=(count // cells,),
        out_shape=[out] + [jax.ShapeDtypeStruct(a.shape, jnp.bfloat16) for a in (far, far)] + [sums],
        in_specs=[pl.BlockSpec(memory_space=pltpu.SMEM)]
        + [row_spec(cells, a, first) for a in (x, grad, own)]
        + [row_spec(cells, far)]
        + [whole_spec(a) for a in whole],
        out_specs=[row_spec(cells, a) for a in (out, far, far)] + [whole_spec(sums)],
        scratch_shapes=[
            pltpu.VMEM((cells * points, chan), jnp.bfloat16),
            pltpu.VMEM((cells * points, chan), jnp.bfloat16),
            pltpu.VMEM((cells * points, hid), jnp.bfloat16),
            pltpu.VMEM((cells * points, hid), jnp.bfloat16),
        ],
        compiler_params=pltpu.CompilerParams(vmem_limit_bytes=VMEM_BYTES),
        cost_estimate=pl.CostEstimate(
            flops=2 * work, bytes_accessed=12 * count * points * chan, transcendentals=0
        ),
        name="slope_rows",
    )(mask, x, grad, own, far, *whole)


def swap(block, axis, mask=1):
    return lax.ppermute(block, axis, [(i, i ^ mask) for i in range(lax.axis_size(axis))])


def pair_sum(block, axis):
    mask = 1
    while mask < lax.axis_size(axis):
        block = block + swap(block, axis, mask)
        mask *= 2
    return block


def scatter_sum(block, axis):
    mask = lax.axis_size(axis) // 2
    place = lax.axis_index(axis)
    while mask:
        low, high = jnp.split(block, 2, axis=-1)
        upper = (place & mask) != 0
        kept = jnp.where(upper, high, low).astype(jnp.float32)
        sent = jnp.where(upper, low, high).astype(jnp.bfloat16)
        block = kept + swap(sent, axis, mask).astype(jnp.float32)
        mask //= 2
    return block


def paired_on_device(
    fresh_input, saved_input, output_grad, expand_weight, reduce_weight, filter_weight, cycle_table
):
    slot_count = fresh_input.shape[2]
    position = lax.axis_index("sp")
    order_table = jnp.arange(slot_count * 2, dtype=jnp.int32)
    here, there = position * slot_count, (1 - position) * slot_count
    cut = functools.partial(lax.dynamic_slice_in_dim, slice_size=slot_count)
    own_cycles, far_cycles = cut(cycle_table, here), cut(cycle_table, there)
    own_orders, far_orders = cut(order_table, here), cut(order_table, there)
    cycle_mask = (own_cycles < NLAT).astype(jnp.float32)
    forward_own, inverse_own = fourier_tables(own_orders, NLAT, NLON)
    forward_far, inverse_far = fourier_tables(far_orders, NLAT, NLON)
    forward_own = interleave(forward_own, slot_count)
    forward_far = interleave(forward_far, slot_count)
    inverse_own = interleave(inverse_own.T, slot_count)
    inverse_far = interleave(inverse_far.T, slot_count)
    filt = filter_weight[0]
    expand = expand_weight[0]
    contract = reduce_weight[0]
    fresh = fresh_input[0, 0]
    saved = saved_input[0, 0]
    points, chan_count = fresh.shape[1:]

    def longitude(x, table):
        return jnp.einsum(
            "jnc,nk->jkc", x, table, preferred_element_type=jnp.float32
        ).astype(jnp.bfloat16)

    half = slot_count // 2
    parts = ((0, half), (half, slot_count))

    def exchange(pieces):
        return [swap(piece, "sp") for piece in pieces]

    def after(values, *before):
        return lax.optimization_barrier((values,) + before)[0]

    saved_send = longitude(saved, forward_far)
    saved_far = swap(saved_send, "sp")
    saved_own = longitude(saved, forward_own)
    fresh_later = after(fresh, saved_own)
    fresh_send = longitude(fresh_later, forward_far)
    fresh_send = [fresh_send[low:high] for low, high in parts]
    fresh_far = [swap(after(fresh_send[0], saved_send), "sp")]
    fresh_own = longitude(fresh_later, forward_own)
    analysis, synthesis = legendre_tables(
        jnp.concatenate([own_cycles, far_cycles]), own_orders, NLAT
    )

    def to_degrees(pieces, table):
        both = jnp.concatenate(pieces, axis=0)
        both = both.reshape(2 * slot_count, slot_count, 2, chan_count)
        return jnp.einsum("tlj,jtrc->trlc", table, both, preferred_element_type=jnp.float32)

    def to_rows(spectra, table, low, high):
        rows = jnp.einsum(
            "tlj,trlc->jtrc", table[:, :, low:high], spectra, preferred_element_type=jnp.float32
        ).astype(jnp.bfloat16)
        return rows.reshape(high - low, 2 * slot_count, chan_count)

    def own_rows(spectra, table):
        return to_rows(spectra, table, 0, slot_count)

    def far_rows(spectra, table):
        rows = to_rows(spectra, table, slot_count, 2 * slot_count)
        return [rows[low:high] for low, high in parts]

    def filtered(spectra):
        real_part = filt[0] * spectra[:, 0] - filt[1] * spectra[:, 1]
        imag_part = filt[0] * spectra[:, 1] + filt[1] * spectra[:, 0]
        return jnp.stack([real_part, imag_part], axis=1).astype(jnp.bfloat16)

    spectra = to_degrees([saved_own, saved_far], analysis)
    saved_filtered = filtered(spectra)
    send_values = far_rows(saved_filtered, synthesis)
    send_values[1] = after(send_values[1], send_values[0])
    came_values = exchange(send_values)
    fresh_far.append(swap(after(fresh_send[1], send_values), "sp"))
    own_values = own_rows(after(saved_filtered, send_values), synthesis)

    slopes = []
    for (low, _), came in zip(parts, came_values):
        slopes.append(
            slope_rows(
                cycle_mask, low, saved, output_grad[0, 0], after(own_values, slopes), came, inverse_own,
                inverse_far, expand, contract,
            )
        )
    grad_mixed, grad_own, grad_send, sums = zip(*slopes)
    grad_far = exchange(grad_send)

    fresh_far = after(fresh_far, grad_send)
    fresh_filtered = filtered(to_degrees([fresh_own] + fresh_far, analysis))
    fresh_send_values = far_rows(fresh_filtered, synthesis)
    fresh_came = exchange(fresh_send_values)
    fresh_own_values = own_rows(fresh_filtered, synthesis)
    sums = scatter_sum(sums[0] + sums[1], "dp")
    scattered = sums
    sums = sums + swap(sums.astype(jnp.bfloat16), "sp").astype(jnp.float32)

    grad_far = after(list(grad_far), fresh_send_values)
    grad_filtered = to_degrees(list(grad_own) + grad_far, synthesis)
    filter_real = jnp.sum(
        grad_filtered[:, 0] * spectra[:, 0] + grad_filtered[:, 1] * spectra[:, 1], axis=0
    )
    filter_imag = jnp.sum(
        grad_filtered[:, 1] * spectra[:, 0] - grad_filtered[:, 0] * spectra[:, 1], axis=0
    )
    grad_spectra = jnp.stack(
        [
            filt[0] * grad_filtered[:, 0] + filt[1] * grad_filtered[:, 1],
            filt[0] * grad_filtered[:, 1] - filt[1] * grad_filtered[:, 0],
        ],
        axis=1,
    ).astype(jnp.bfloat16)
    send_coeffs = far_rows(after(grad_spectra, scattered), analysis)
    send_coeffs[1] = after(send_coeffs[1], send_coeffs[0])
    came_coeffs = exchange(send_coeffs)
    fresh_came[0] = after(fresh_came[0], send_coeffs)
    own_coeffs = own_rows(after(grad_spectra, send_coeffs), analysis)
    filter_grad = pair_sum(jnp.stack([filter_real, filter_imag]), "dp")
    fresh_came[1] = after(fresh_came[1], filter_grad, sums)
    filter_grad = pair_sum(filter_grad, "sp")

    def joined(pieces):
        whole = jnp.zeros((1, 1) + fresh.shape, jnp.bfloat16)
        for (low, _), piece in zip(parts, pieces):
            whole = lax.dynamic_update_slice(whole, piece[None, None], (0, 0, low, 0, 0))
        return whole

    blocks, back_pieces = [], []
    for at, (low, high) in enumerate(parts):
        blocks.append(
            value_rows(
                cycle_mask, low, fresh, after(fresh_own_values, back_pieces), fresh_came[at],
                inverse_own, inverse_far, expand, contract,
            )
        )
        grad_tokens = jnp.einsum(
            "jkc,nk->jnc", own_coeffs[low:high], forward_own, preferred_element_type=jnp.float32
        ) + jnp.einsum(
            "jkc,nk->jnc", after(came_coeffs[at], blocks), forward_far, preferred_element_type=jnp.float32
        )
        piece = (grad_mixed[at].astype(jnp.float32) + grad_tokens) * cycle_mask[low:high, None, None]
        back_pieces.append(piece.astype(jnp.bfloat16))
    next_input = joined([from_behind(block, "pipe", 1) for block in blocks])
    first_back = from_behind(back_pieces[0], "pipe", -1)
    back_pieces = [first_back, from_behind(after(back_pieces[1], first_back), "pipe", -1)]
    return (
        next_input,
        joined(back_pieces),
        sums[0][None],
        sums[1].T[None],
        filter_grad[None],
    )


def solution(mesh):
    groups = mesh.shape["dp"]
    paired = mesh.shape["sp"] == 2 and groups & (groups - 1) == 0
    return jax.shard_map(
        paired_on_device if paired else on_device,
        mesh=mesh,
        in_specs=(
            P("pipe", "dp", "sp", None, None),
            P("pipe", "dp", "sp", None, None),
            P("pipe", "dp", "sp", None, None),
            P("pipe", None, None),
            P("pipe", None, None),
            P("pipe", None, None, None),
            P(),
        ),
        out_specs=(
            P("pipe", "dp", "sp", None, None),
            P("pipe", "dp", "sp", None, None),
            P("pipe", None, "dp"),
            P("pipe", "dp", None),
            P("pipe", None, None, None),
        ),
        check_vma=False,
    )
```
